32 devices in a mesh: dp: 16 (over z, y, x), tensor: 2 (over core).
Axes of the slice: x: 2, y: 2, z: 4, core: 2. Of those that a mesh axis runs over, the one named last changes fastest.
Arguments:
- inputs: bfloat16 [8192, 2048], P('dp'), may hold values from -6 to 6
- gamma_first: bfloat16 [2048], replicated, may hold values from 0.099609375 to 1.8984375
- beta_first: bfloat16 [2048], replicated, may hold values from -4 to 4
- heads_weight: bfloat16 [2048, 3, 2048], P('dp', None, 'tensor'), may hold values from -0.125 to 0.125
- output_weight: bfloat16 [2048, 2048], P('dp', 'tensor'), may hold values from -0.5 to 0.5
- output_bias: bfloat16 [2048], replicated, may hold values from -4 to 4
- gamma_second: bfloat16 [2048], replicated, may hold values from 0.099609375 to 1.8984375
- beta_second: bfloat16 [2048], replicated, may hold values from -4 to 4
- expand_weight: bfloat16 [2048, 8192], P('dp', 'tensor'), may hold values from -0.125 to 0.125
- expand_bias: bfloat16 [8192], P('tensor'), may hold values from -6 to 6
- reduce_weight: bfloat16 [2048, 8192], P('dp', 'tensor'), may hold values from -0.0625 to 0.0625
- reduce_bias: bfloat16 [2048], replicated, may hold values from -4 to 4
- group_sizes: int32 [32], P('dp'), may hold values from 4 to 16, as said below
- prefix_lengths: int32 [32], P('dp'), may hold values from 32 to 128, as said below
- solution_lengths: int32 [32, 16], P('dp'), may hold values from 1 to 221, as said below
- cotangent: bfloat16 [8192, 2048], P('dp'), may hold values from -6 to 6
Outputs:
- outputs: bfloat16 [8192, 2048], P('dp')
- input_gradient: bfloat16 [8192, 2048], P('dp')
- gamma_first_gradient: float32 [2048], P('dp')
- beta_first_gradient: float32 [2048], P('dp')
- heads_weight_gradient: float32 [2048, 3, 2048], P('dp', None, 'tensor')
- output_weight_gradient: float32 [2048, 2048], P('dp', 'tensor')
- output_bias_gradient: float32 [2048], P('dp')
- gamma_second_gradient: float32 [2048], P('dp')
- beta_second_gradient: float32 [2048], P('dp')
- expand_weight_gradient: float32 [2048, 8192], P('dp', 'tensor')
- expand_bias_gradient: float32 [2, 4096], P('tensor', 'dp')
- reduce_weight_gradient: float32 [2048, 8192], P('dp', 'tensor')
- reduce_bias_gradient: float32 [2048], P('dp')
The draws below stay inside these ranges and needn't reach their ends.
Inputs may be any that keep to these rules, and one draw needn't show every extreme that they name: Each group has group_sizes solutions. `prefix_lengths`: A group's prefix and its first group_sizes solutions together take at most 256 token slots. `solution_lengths`: only a group's first group_sizes entries are used. The groups of a block fill at most 512 slots, and on at least one block exactly 512.
All inputs are finite; a program needn't handle non-finite values.
Results may differ from the reference program's by a relative error of at most 0.017.
Values may be sent and summed in bfloat16 or wider, within the bound.
No kernel may reach another device: no remote copies, remote signals or barrier semaphores. Data moves between devices by JAX's collectives and lax.ppermute only.
A program may use at most 384 MiB of HBM per device.

```python
import jax
import jax.numpy as jnp
from jax import lax

D = 2048
HEADS = 16
HEAD = 128
FF = 8192
TOK_DEV = 512
GROUPS_DEV = 2
SOLS = 16
GROUPS = 32
TOKENS = 8192
N_DP = 16
N_TENSOR = 2


def arrange(key):
    folded = jax.random.fold_in(key, 11)
    subkeys = jax.random.split(folded, 6)
    group_share = TOK_DEV // GROUPS_DEV
    group_ids = jnp.arange(GROUPS, dtype=jnp.int32)
    first_group = group_ids == 0
    last_group = group_ids == GROUPS - 1
    counts = jax.random.randint(subkeys[0], (GROUPS,), 4, 17, dtype=jnp.int32)
    counts = jnp.where(first_group, 4, counts).astype(jnp.int32)
    prefix = jax.random.randint(subkeys[1], (GROUPS,), group_share // 8, group_share // 2 + 1, dtype=jnp.int32)
    prefix = jnp.where(first_group, group_share // 8, prefix)
    prefix = jnp.where(last_group, group_share // 2, prefix).astype(jnp.int32)
    remaining = group_share - prefix
    slack_room = jax.random.randint(subkeys[2], (GROUPS,), 0, remaining // 2 + 1, dtype=jnp.int32)
    devices = GROUPS // GROUPS_DEV
    fullest = jax.random.randint(subkeys[3], (), 0, devices, dtype=jnp.int32)
    owner_device = group_ids // GROUPS_DEV
    used_room = remaining - jnp.where((owner_device == fullest) | first_group, 0, slack_room)
    weights = jax.random.randint(subkeys[4], (GROUPS, SOLS), 1, 5, dtype=jnp.int32)
    slot_index = jnp.arange(SOLS, dtype=jnp.int32)[None, :]
    live_slots = slot_index < counts[:, None]
    weights = jnp.where(live_slots, weights, 0)
    spread = (used_room - counts)[:, None] * weights // jnp.sum(weights, axis=1, keepdims=True).astype(jnp.int32)
    lengths = jnp.where(live_slots, 1 + spread, 0).astype(jnp.int32)
    remainder = (used_room - jnp.sum(lengths, axis=1)).astype(jnp.int32)
    lengths = lengths + jnp.where(slot_index == counts[:, None] - 1, remainder[:, None], 0)
    unused = jax.random.randint(subkeys[5], (GROUPS, SOLS), 1, group_share // 8 + 1, dtype=jnp.int32)
    lengths = jnp.where(live_slots, lengths, unused).astype(jnp.int32)
    longest = group_share - group_share // 8 - 3
    special = jnp.where(slot_index < 3, 1, jnp.where(slot_index == 3, longest, unused[0:1, :])).astype(jnp.int32)
    lengths = jnp.where(first_group[:, None], special, lengths).astype(jnp.int32)
    return (counts, prefix, lengths)


def draw_group_sizes(key, part):
    return arrange(key)[0]


def draw_prefix_lengths(key, part):
    return arrange(key)[1]


def draw_solution_lengths(key, part):
    return arrange(key)[2]


def strengthened(array, rng, source, target, shards_of, factor):
    owner, partner = [(jnp.arange(array.shape[dim]) // (array.shape[dim] // shards_of)).reshape([-1 if axis == dim else 1 for axis in range(array.ndim)]) for dim in (source, target)]
    chosen = jax.random.permutation(rng, shards_of)[partner]
    strong = (owner == chosen) | (owner == (partner + shards_of // 2) % shards_of)
    return jnp.where(strong, factor * array, array)


def shard_levels(stream_key, shape, cuts, smallest, top_value):
    def one(axis_at, shards_of):
        draws = jax.random.uniform(jax.random.fold_in(jax.random.fold_in(stream_key, 6), axis_at), (shards_of,), jnp.float32, smallest / len(cuts), top_value / len(cuts))
        return jnp.repeat(jnp.exp(draws), shape[axis_at] // shards_of).reshape((-1,) + (1,) * (len(shape) - axis_at - 1))

    level = one(*cuts[0])
    for cut in cuts[1:]:
        level = level * one(*cut)
    return level


def noise(own_key, shape, deviation, most, cuts=(), held_as=jnp.bfloat16):
    drawn = deviation * jax.random.normal(own_key, shape, jnp.float32)
    if cuts:
        drawn = drawn * shard_levels(own_key, shape, cuts, -0.22, 0.18)
    return jnp.clip(drawn, -most, most).astype(held_as)


def heavy_noise(stream_key, dims, deviation, most, shards, heavy, held_as=jnp.bfloat16):
    values = deviation * jax.random.normal(stream_key, dims, jnp.float32)
    if shards:
        values = values * shard_levels(stream_key, dims, shards, -0.22, 0.18)
    return jnp.clip(strengthened(values, jax.random.fold_in(stream_key, 3), *heavy), -most, most).astype(held_as)


def setup_inputs(seed: int = 0) -> dict:
    arg_keys = jax.random.split(jax.random.key(seed), 17)
    inputs = noise(arg_keys[0], (TOKENS, D), 1.0, 6.0, ((0, 16),))
    gamma_first = jnp.clip(1.0 + 0.18 * jax.random.normal(arg_keys[1], (D,), jnp.float32), 0.099609375, 1.8984375).astype(jnp.bfloat16)
    beta_first = noise(arg_keys[2], (D,), 0.3, 4.0)
    heads_weight = noise(arg_keys[3], (D, 3, D), D ** -0.5, 0.125, ((0, 16), (2, 2)))
    output_weight = noise(arg_keys[4], (D, D), (D // 16) ** -0.5, 0.5, ((0, 16), (1, 2)))
    output_bias = noise(arg_keys[5], (D,), 0.3, 4.0)
    gamma_second = jnp.clip(1.0 + 0.18 * jax.random.normal(arg_keys[6], (D,), jnp.float32), 0.099609375, 1.8984375).astype(jnp.bfloat16)
    beta_second = noise(arg_keys[7], (D,), 0.3, 4.0)
    expand_weight = noise(arg_keys[8], (D, FF), D ** -0.5, 0.125, ((0, 16), (1, 2)))
    expand_bias = noise(arg_keys[9], (FF,), 0.5, 6.0, ((0, 2),))
    reduce_weight = noise(arg_keys[10], (D, FF), FF ** -0.5, 0.0625, ((0, 16), (1, 2)))
    reduce_bias = noise(arg_keys[11], (D,), 0.3, 4.0)
    group_sizes = draw_group_sizes(jax.random.fold_in(arg_keys[16], 71), 0)
    prefix_lengths = draw_prefix_lengths(jax.random.fold_in(arg_keys[16], 71), 0)
    solution_lengths = draw_solution_lengths(jax.random.fold_in(arg_keys[16], 71), 0)
    cotangent = heavy_noise(arg_keys[15], (TOKENS, D), 1.0, 6.0, ((0, 16),), (0, 1, 16, 2.0))
    return dict(inputs=inputs, gamma_first=gamma_first, beta_first=beta_first, heads_weight=heads_weight, output_weight=output_weight, output_bias=output_bias, gamma_second=gamma_second, beta_second=beta_second, expand_weight=expand_weight, expand_bias=expand_bias, reduce_weight=reduce_weight, reduce_bias=reduce_bias, group_sizes=group_sizes, prefix_lengths=prefix_lengths, solution_lengths=solution_lengths, cotangent=cotangent)


@jax.custom_vjp
def low(v):
    return lax.optimization_barrier(v.astype(jnp.bfloat16)).astype(jnp.float32)

@jax.custom_vjp
def low_back(v):
    return v

def low_keep(v):
    return (low(v), None)

def low_pass(kept, grad):
    return (grad,)

def back_keep(v):
    return (v, None)

def back_low(kept, grad):
    return (low(grad),)
low.defvjp(low_keep, low_pass)
low_back.defvjp(back_keep, back_low)

def layout(group_sizes, prefix_lengths, solution_lengths, row_count):
    entries = solution_lengths.shape[1]
    position = jnp.arange(entries, dtype=jnp.int32)
    counted = jnp.where(position[None, :] < group_sizes[:, None], solution_lengths, 0).astype(jnp.int32)
    pieces = jnp.concatenate([prefix_lengths[:, None].astype(jnp.int32), counted], axis=1).reshape(-1)
    bounds = jnp.cumsum(pieces).astype(jnp.int32)
    slot_index = jnp.arange(row_count, dtype=jnp.int32)
    piece_index = lax.optimization_barrier(jnp.sum((slot_index[:, None] >= bounds[None, :]).astype(jnp.int32), axis=1)).astype(jnp.int32)
    live_rows = piece_index < pieces.shape[0]
    group_index = piece_index // (entries + 1)
    opening = piece_index % (entries + 1) == 0
    same_group = (group_index[:, None] == group_index[None, :]) & live_rows[:, None] & live_rows[None, :]
    causal = slot_index[None, :] <= slot_index[:, None]
    visible = opening[None, :] | (piece_index[:, None] == piece_index[None, :])
    allowed = (slot_index[:, None] == slot_index[None, :]) | same_group & causal & visible
    return (allowed, live_rows)

def normalize(values, gain_vector, shift_vector):
    center = values - lax.optimization_barrier(jnp.mean(values, axis=-1, keepdims=True))
    spread = lax.optimization_barrier(jnp.mean(center * center, axis=-1, keepdims=True))
    return center * lax.rsqrt(spread + 1e-05) * gain_vector + shift_vector

def block_forward(residual, gamma_first, beta_first, heads_weight, output_weight, output_bias, gamma_second, beta_second, expand_weight, expand_bias, reduce_weight, reduce_bias, allowed, live_mask):
    highest = lax.Precision.HIGHEST
    row_count = residual.shape[0]
    first_low = low(normalize(residual, gamma_first, beta_first))
    projected = low(low_back(jnp.einsum('td,dch->tch', first_low, heads_weight, precision=highest)))
    queries = projected[:, 0].reshape(row_count, HEADS, HEAD)
    keyset = projected[:, 1].reshape(row_count, HEADS, HEAD)
    valueset = projected[:, 2].reshape(row_count, HEADS, HEAD)
    raw_scores = low_back(jnp.einsum('qhe,khe->hqk', queries, keyset, precision=highest) * HEAD ** (-0.5))
    scores = jnp.where(allowed[None], raw_scores, -1e+30)
    soft_low = low(jax.nn.softmax(scores, axis=-1))
    mixed_heads = low(low_back(jnp.einsum('hqk,khe->qhe', soft_low, valueset, precision=highest).reshape(row_count, HEADS * HEAD)))
    middle = residual + low_back(jnp.einsum('te,de->td', mixed_heads, output_weight, precision=highest)) + output_bias
    second_low = low(normalize(middle, gamma_second, beta_second))
    hidden_sum = low_back(jnp.dot(second_low, expand_weight, precision=highest)) + expand_bias
    hidden_low = low(jax.nn.gelu(hidden_sum, approximate=True))
    branch = low_back(jnp.einsum('tf,df->td', hidden_low, reduce_weight, precision=highest)) + reduce_bias
    return live_mask[:, None] * (middle + branch)

def reference(inputs, gamma_first, beta_first, heads_weight, output_weight, output_bias, gamma_second, beta_second, expand_weight, expand_bias, reduce_weight, reduce_bias, group_sizes, prefix_lengths, solution_lengths, cotangent):
    params = tuple((member.astype(jnp.float32) for member in (gamma_first, beta_first, heads_weight, output_weight, output_bias, gamma_second, beta_second, expand_weight, expand_bias, reduce_weight, reduce_bias)))
    blocks_in = inputs.astype(jnp.float32).reshape(N_DP, TOK_DEV, D)
    blocks_tangent = cotangent.astype(jnp.float32).reshape(N_DP, TOK_DEV, D)
    sizes_block = group_sizes.reshape(N_DP, GROUPS_DEV)
    prefix_block = prefix_lengths.reshape(N_DP, GROUPS_DEV)
    length_block = solution_lengths.reshape(N_DP, GROUPS_DEV, SOLS)

    def one_block(running, block_item):
        block_rows, block_tangent, block_sizes, block_prefix, block_lengths = block_item
        allowed, live_rows = layout(block_sizes, block_prefix, block_lengths, TOK_DEV)
        live_mask = live_rows.astype(jnp.float32)

        def forward(residual, *weights):
            return block_forward(residual, *weights, allowed, live_mask)
        produced, pullback = jax.vjp(forward, block_rows, *params)
        gradients = pullback(block_tangent)
        updated = tuple((prior + fresh for prior, fresh in zip(running, gradients[1:])))
        return (updated, (produced.astype(jnp.bfloat16), gradients[0].astype(jnp.bfloat16)))
    start_sums = tuple((jnp.zeros(member.shape, jnp.float32) for member in params))
    totals, (produced, input_blocks) = lax.scan(one_block, start_sums, (blocks_in, blocks_tangent, sizes_block, prefix_block, length_block))
    outputs = produced.reshape(N_DP * TOK_DEV, D)
    input_gradient = input_blocks.reshape(N_DP * TOK_DEV, D)
    return (outputs, input_gradient, totals[0], totals[1], totals[2], totals[3], totals[4], totals[5], totals[6], totals[7], totals[8].reshape(N_TENSOR, FF // N_TENSOR), totals[9], totals[10])
```

```python
import functools

import jax
import jax.numpy as jnp
from jax import lax
from jax.experimental import pallas as pl
from jax.experimental.pallas import tpu as pltpu
from jax.sharding import Mesh
from jax.sharding import PartitionSpec as P

HEAD = 128
WINDOW = 256
CHUNK = 128
SCALE = HEAD**-0.5
ALL = ("z", "y", "x", "c")
BF = jnp.bfloat16
F32 = jnp.float32
ACROSS = (((1,), (1,)), ((), ()))
ROWS = (((0,), (0,)), ((), ()))
PLAIN = (((1,), (0,)), ((), ()))


def dot(a, b, dims=PLAIN):
    return lax.dot_general(a, b, dims, preferred_element_type=F32)


def add_dots(pairs, dims=PLAIN):
    total = None
    for a, b in pairs:
        part = dot(a, b, dims)
        total = part if total is None else total + part
    return total


def pairs_of(depth, route):
    def flat(z, y, x, c):
        return ((z * 2 + y) * 2 + x) * 2 + c

    found = []
    for z in range(depth):
        for y in range(2):
            for x in range(2):
                for c in range(2):
                    goal = route(y, x, c)
                    if goal is not None:
                        found.append((flat(z, y, x, c), flat(z, *goal)))
    return found


def bounds_of(group_sizes, prefix_lengths, solution_lengths, row_count):
    entries = solution_lengths.shape[1]
    position = jnp.arange(entries, dtype=jnp.int32)
    counted = jnp.where(position[None, :] < group_sizes[:, None], solution_lengths, 0)
    pieces = jnp.concatenate([prefix_lengths[:, None], counted], axis=1)
    flat = pieces.reshape(-1)
    count = flat.shape[0]
    index = jnp.arange(count, dtype=jnp.int32)
    ends = jnp.sum(jnp.where(index[None, :] <= index[:, None], flat[None, :], 0), axis=1)
    slot = jnp.arange(row_count, dtype=jnp.int32)
    passed = slot[:, None] >= ends[None, :]
    piece_start = jnp.max(jnp.where(passed, ends[None, :], 0), axis=1)
    group_end = ends.reshape(pieces.shape)[:, -1]
    over = slot[:, None] >= group_end[None, :]
    group_start = jnp.max(jnp.where(over, group_end[None, :], 0), axis=1)
    group_index = jnp.sum(over.astype(jnp.int32), axis=1)
    member = group_index[:, None] == jnp.arange(pieces.shape[0], dtype=jnp.int32)[None, :]
    prefix_end = group_start + jnp.sum(jnp.where(member, prefix_lengths[None, :], 0), axis=1)
    live = slot < ends[-1]
    piece_start = jnp.where(live, piece_start, slot)
    group_start = jnp.where(live, group_start, slot)
    prefix_end = jnp.where(live, prefix_end, slot)
    return jnp.stack([group_start, prefix_end, piece_start], axis=1), live


def key_range(i):
    return max(0, i * CHUNK - WINDOW), (i + 1) * CHUNK


def allowed_tile(info, i, lo, hi):
    rows = info[i * CHUNK : (i + 1) * CHUNK, :]
    start, stop, piece = rows[:, 0:1], rows[:, 1:2], rows[:, 2:3]
    s = lax.broadcasted_iota(jnp.int32, (CHUNK, hi - lo), 0) + i * CHUNK
    t = lax.broadcasted_iota(jnp.int32, (CHUNK, hi - lo), 1) + lo
    return (t <= s) & ((t >= piece) | ((t >= start) & (t < stop)))


def attend_kernel(info_ref, p0_ref, p1_ref, o0_ref, o1_ref):
    block, width = p0_ref.shape
    width = width // 3
    info = info_ref[...]
    for i in range(block // CHUNK):
        lo, hi = key_range(i)
        allowed = allowed_tile(info, i, lo, hi)
        rows = slice(i * CHUNK, (i + 1) * CHUNK)
        for p_ref, o_ref in ((p0_ref, o0_ref), (p1_ref, o1_ref)):
            for h in range(width // HEAD):
                q = p_ref[rows, h * HEAD : (h + 1) * HEAD]
                k = p_ref[lo:hi, width + h * HEAD : width + (h + 1) * HEAD]
                v = p_ref[lo:hi, 2 * width + h * HEAD : 2 * width + (h + 1) * HEAD]
                scores = jnp.where(allowed, dot(q, k, ACROSS) * SCALE, -1e30)
                e = jnp.exp(scores - jnp.max(scores, axis=-1, keepdims=True))
                soft = e / jnp.sum(e, axis=-1, keepdims=True)
                o_ref[rows, h * HEAD : (h + 1) * HEAD] = dot(soft.astype(BF), v).astype(BF)


def attend_back_kernel(info_ref, p0_ref, p1_ref, g0_ref, g1_ref, d0_ref, d1_ref, dk_ref, dv_ref):
    block, width = p0_ref.shape
    width = width // 3
    info = info_ref[...]
    masks = []
    for i in range(block // CHUNK):
        lo, hi = key_range(i)
        masks.append(allowed_tile(info, i, lo, hi))
    for p_ref, g_ref, d_ref in ((p0_ref, g0_ref, d0_ref), (p1_ref, g1_ref, d1_ref)):
        for h in range(width // HEAD):
            dk_ref[...] = jnp.zeros_like(dk_ref)
            dv_ref[...] = jnp.zeros_like(dv_ref)
            qs = slice(h * HEAD, (h + 1) * HEAD)
            ks = slice(width + h * HEAD, width + (h + 1) * HEAD)
            vs = slice(2 * width + h * HEAD, 2 * width + (h + 1) * HEAD)
            for i in range(block // CHUNK):
                lo, hi = key_range(i)
                rows = slice(i * CHUNK, (i + 1) * CHUNK)
                q = p_ref[rows, qs]
                k = p_ref[lo:hi, ks]
                v = p_ref[lo:hi, vs]
                g = g_ref[rows, qs]
                scores = jnp.where(masks[i], dot(q, k, ACROSS) * SCALE, -1e30)
                e = jnp.exp(scores - jnp.max(scores, axis=-1, keepdims=True))
                soft = e / jnp.sum(e, axis=-1, keepdims=True)
                back = dot(g, v, ACROSS)
                low = (soft * (back - jnp.sum(soft * back, axis=-1, keepdims=True))).astype(BF)
                d_ref[rows, qs] = (dot(low, k) * SCALE).astype(BF)
                dk_ref[lo:hi, :] += dot(low, q, ROWS)
                dv_ref[lo:hi, :] += dot(soft.astype(BF), g, ROWS)
            d_ref[:, ks] = (dk_ref[...] * SCALE).astype(BF)
            d_ref[:, vs] = dv_ref[...].astype(BF)


def attend(info, p0, p1, block):
    rows, width = p0.shape
    spec = lambda n: pl.BlockSpec((block, n), lambda b: (b, 0))
    out = jax.ShapeDtypeStruct((rows, width // 3), BF)
    return pl.pallas_call(
        attend_kernel,
        grid=(rows // block,),
        in_specs=[spec(info.shape[1]), spec(width), spec(width)],
        out_specs=[spec(width // 3)] * 2,
        out_shape=[out, out],
        compiler_params=pltpu.CompilerParams(vmem_limit_bytes=32 << 20),
        cost_estimate=pl.CostEstimate(
            flops=4 * rows * block * width, bytes_accessed=4 * rows * width * 2, transcendentals=rows * block * 4
        ),
        name="attend",
    )(info, p0, p1)


def attend_back(info, p0, p1, g0, g1, block):
    rows, width = p0.shape
    spec = lambda n: pl.BlockSpec((block, n), lambda b: (b, 0))
    out = jax.ShapeDtypeStruct((rows, width), BF)
    return pl.pallas_call(
        attend_back_kernel,
        grid=(rows // block,),
        in_specs=[spec(info.shape[1]), spec(width), spec(width), spec(width // 3), spec(width // 3)],
        out_specs=[spec(width)] * 2,
        out_shape=[out, out],
        scratch_shapes=[pltpu.VMEM((block, HEAD), F32)] * 2,
        compiler_params=pltpu.CompilerParams(vmem_limit_bytes=32 << 20),
        cost_estimate=pl.CostEstimate(
            flops=10 * rows * block * width, bytes_accessed=8 * rows * width * 2, transcendentals=rows * block * 4
        ),
        name="attend_back",
    )(info, p0, p1, g0, g1)


def normalize(values, gain_vector, shift_vector):
    center = values - jnp.mean(values, axis=-1, keepdims=True)
    spread = jnp.mean(center * center, axis=-1, keepdims=True)
    return center * lax.rsqrt(spread + 1e-05) * gain_vector + shift_vector


def smooth(values):
    return jax.nn.gelu(values, approximate=True)


def body(
    depth,
    inputs,
    gamma_first,
    beta_first,
    heads_weight,
    output_weight,
    output_bias,
    gamma_second,
    beta_second,
    expand_weight,
    expand_bias,
    reduce_weight,
    reduce_bias,
    group_sizes,
    prefix_lengths,
    solution_lengths,
    cotangent,
):
    block, model = inputs.shape
    zi, yi, xi, ci = (lax.axis_index(a) for a in ALL)
    plane = yi * 2 + xi
    own = xi == ci
    send = lambda v, route: lax.ppermute(v, ALL, pairs_of(depth, route))
    wide = lambda v: v.astype(F32)

    def near_of(v):
        return send(v, lambda y, x, c: (y, x, c) if c == x else (y, 1 - x, 1 - c))

    def far_of(v):
        return send(v, lambda y, x, c: (1 - y, x, c) if c == x else (1 - y, 1 - x, 1 - c))

    def spread(v):
        half = v.shape[0] // 2
        over_y = send(v, lambda y, x, c: (1 - y, x, c) if c == x else None)
        over_x = send(v, lambda y, x, c: (y, 1 - x, c) if c == x else None)
        near = jnp.where(own, v, over_x)
        first_half = send(over_x[:half], lambda y, x, c: (1 - y, x, c) if c != x else None)
        second_half = send(over_y[half:], lambda y, x, c: (y, 1 - x, c) if c == x else None)
        far = jnp.where(own, over_y, jnp.concatenate([first_half, second_half], axis=0))
        return jnp.concatenate([near, far], axis=0)

    def collect(v):
        near, far = v[:block], v[block:]
        half = block // 2
        a = send(far[:half], lambda y, x, c: (1 - y, x, c) if c != x else None)
        b = send(far[half:], lambda y, x, c: (y, 1 - x, c) if c != x else None)
        send_x = jnp.concatenate([(wide(near[:half]) + wide(a)).astype(BF), near[half:]], axis=0)
        send_y = jnp.concatenate([far[:half], (wide(far[half:]) + wide(b)).astype(BF)], axis=0)
        from_x = send(send_x, lambda y, x, c: (y, 1 - x, c) if c != x else None)
        from_y = send(send_y, lambda y, x, c: (1 - y, x, c) if c == x else None)
        return wide(near) + wide(from_x) + wide(from_y)

    def from_owner(v):
        return jnp.where(own, v, send(v, lambda y, x, c: (y, x, 1 - c) if c == x else None))

    def shuffle(v):
        take = lambda k: lax.dynamic_index_in_dim(v, plane ^ k, 0, keepdims=False)
        mine = take(0)
        by_x = send(take(1), lambda y, x, c: (y, 1 - x, c))
        by_y = send(take(2), lambda y, x, c: (1 - y, x, c))
        by_both = send(take(3), lambda y, x, c: (1 - y, 1 - x, c))
        even, low = xi == 0, yi == 0
        a0, a1 = jnp.where(even, mine, by_x), jnp.where(even, by_x, mine)
        b0, b1 = jnp.where(even, by_y, by_both), jnp.where(even, by_both, by_y)
        return [
            jnp.where(low, a0, b0),
            jnp.where(low, a1, b1),
            jnp.where(low, b0, a0),
            jnp.where(low, b1, a1),
        ]

    def gather(v):
        full = lax.all_gather(v, ("c", "z"), axis=0, tiled=True)
        return full.reshape(2, full.shape[0] // 2, full.shape[1])

    def scatter(v):
        return lax.psum_scatter(v.reshape(-1, v.shape[-1]), ("c", "z"), scatter_dimension=0, tiled=True)

    shard, _, local = heads_weight.shape
    part = local // 4
    inner = expand_weight.shape[1] // 4
    heads_in = heads_weight.reshape(shard, 3, 4, part).transpose(2, 0, 1, 3).reshape(4, shard, 3 * part)
    heads_all = gather(jnp.concatenate(shuffle(heads_in), axis=0))
    out_in = output_weight.reshape(shard, 4, part).transpose(1, 0, 2)
    expand_in = expand_weight.reshape(shard, 4, inner).transpose(1, 0, 2)
    reduce_in = reduce_weight.reshape(shard, 4, inner).transpose(1, 0, 2)
    rest = shuffle(jnp.concatenate([out_in, expand_in, reduce_in], axis=2))
    out_all = gather(jnp.concatenate([r[:, :part] for r in rest], axis=0))
    expand_all = gather(jnp.concatenate([r[:, part : part + inner] for r in rest], axis=0))
    reduce_all = gather(jnp.concatenate([r[:, part + inner :] for r in rest], axis=0))
    bias_mine = lax.dynamic_slice_in_dim(expand_bias, plane * inner, inner).reshape(1, inner)
    bias_other = send(bias_mine, lambda y, x, c: (y, x, 1 - c))
    bias = [wide(jnp.where(ci == k, bias_mine, bias_other)) for k in range(2)]

    info, live = bounds_of(group_sizes, prefix_lengths, solution_lengths, block)
    info = jnp.pad(info, ((0, 0), (0, 5)))
    live_mask = wide(live)[:, None]
    info_two = jnp.concatenate([near_of(info), far_of(info)], axis=0)
    gain_first, shift_first = wide(gamma_first), wide(beta_first)
    gain_second, shift_second = wide(gamma_second), wide(beta_second)
    residual = wide(inputs)
    first_own = normalize(residual, gain_first, shift_first).astype(BF)
    first = jnp.concatenate([near_of(first_own), far_of(first_own)], axis=0)
    upstream = live_mask * wide(cotangent)
    upstream_own = upstream.astype(BF)
    upstream_low = jnp.concatenate([near_of(upstream_own), far_of(upstream_own)], axis=0)
    reduce_bias_gradient = jnp.sum(upstream, axis=0)

    projected = [dot(first, heads_all[k]).astype(BF) for k in range(2)]
    mixed = attend(info_two, projected[0], projected[1], block)
    attended = collect(add_dots([(mixed[k], out_all[k]) for k in range(2)], ACROSS).astype(BF))
    middle = residual + attended + wide(output_bias)
    second_own = normalize(middle, gain_second, shift_second).astype(BF)
    second = spread(second_own)
    hidden = [dot(second, expand_all[k]) + bias[k] for k in range(2)]
    activated = [smooth(h).astype(BF) for h in hidden]
    reduce_terms = jnp.stack([dot(upstream_low, activated[k], ROWS).astype(BF) for k in range(2)])
    reduce_part = scatter(reduce_terms)

    hidden_back = [dot(upstream_low, reduce_all[k]) for k in range(2)]
    sum_back = [jax.vjp(smooth, hidden[k])[1](hidden_back[k])[0] for k in range(2)]
    sum_low = [s.astype(BF) for s in sum_back]
    expand_bias_gradient = jnp.stack([jnp.sum(s, axis=0) for s in sum_back])
    second_back = collect(add_dots([(sum_low[k], expand_all[k]) for k in range(2)], ACROSS).astype(BF))
    expand_terms = jnp.stack([dot(second, sum_low[k], ROWS).astype(BF) for k in range(2)])
    expand_part = scatter(expand_terms)
    branch = collect(add_dots([(activated[k], reduce_all[k]) for k in range(2)], ACROSS).astype(BF))
    outputs = from_owner((live_mask * (middle + branch + wide(reduce_bias))).astype(BF))

    _, second_pullback = jax.vjp(normalize, middle, gain_second, shift_second)
    middle_part, gamma_second_gradient, beta_second_gradient = second_pullback(second_back)
    middle_back = upstream + middle_part
    output_bias_gradient = jnp.sum(middle_back, axis=0)
    middle_low = spread(middle_back.astype(BF))

    mixed_back = [dot(middle_low, out_all[k]).astype(BF) for k in range(2)]
    projected_back = attend_back(info_two, projected[0], projected[1], mixed_back[0], mixed_back[1], block)
    heads_terms = jnp.stack(
        [
            jnp.concatenate(
                [dot(first, projected_back[k], ROWS).astype(BF), dot(middle_low, mixed[k], ROWS).astype(BF)], axis=1
            )
            for k in range(2)
        ]
    )
    heads_part = scatter(heads_terms)
    first_back = collect(add_dots([(projected_back[k], heads_all[k]) for k in range(2)], ACROSS).astype(BF))
    _, first_pullback = jax.vjp(normalize, residual, gain_first, shift_first)
    input_part, gamma_first_gradient, beta_first_gradient = first_pullback(first_back)
    input_gradient = from_owner((middle_back + input_part).astype(BF))

    rows_out = lambda v: v.reshape(4, shard, v.shape[-1])
    reduce_gradient = wide(jnp.concatenate(shuffle(rows_out(reduce_part)), axis=1))
    expand_gradient = wide(jnp.concatenate(shuffle(rows_out(expand_part)), axis=1))
    heads_out = shuffle(rows_out(heads_part))
    heads_gradient = wide(jnp.stack([h[:, : 3 * part].reshape(shard, 3, part) for h in heads_out], axis=2))
    heads_gradient = heads_gradient.reshape(shard, 3, local)
    output_gradient = wide(jnp.concatenate([h[:, 3 * part :] for h in heads_out], axis=1))

    vectors = jnp.stack(
        [
            gamma_first_gradient,
            beta_first_gradient,
            output_bias_gradient,
            gamma_second_gradient,
            beta_second_gradient,
            reduce_bias_gradient,
        ]
    )
    vectors = jnp.where(own, vectors, 0.0)
    placed = lax.dynamic_update_slice(jnp.zeros((2, 4 * inner), F32), expand_bias_gradient, (0, plane * inner))
    sums = jnp.concatenate([vectors.reshape(-1), placed.reshape(-1)]).reshape(-1, 128)
    for route in (
        lambda y, x, c: (y, x, 1 - c),
        lambda y, x, c: (y, 1 - x, c),
        lambda y, x, c: (1 - y, x, c),
    ):
        sums = sums + send(sums, route)
    step = 1
    while step < depth:
        sums = sums + lax.ppermute(sums, "z", [(i, i ^ step) for i in range(depth)])
        step *= 2
    flat = sums.reshape(-1)
    index = zi * 4 + plane
    vectors = lax.dynamic_slice_in_dim(flat[: 6 * model].reshape(6, model), index * shard, shard, axis=1)
    placed = flat[6 * model :].reshape(2, 4 * inner)
    count = 4 * inner // (4 * depth)
    expand_bias_gradient = lax.dynamic_slice(placed, (ci, index * count), (1, count))
    return (
        outputs,
        input_gradient,
        vectors[0],
        vectors[1],
        heads_gradient,
        output_gradient,
        vectors[2],
        vectors[3],
        vectors[4],
        expand_gradient,
        expand_bias_gradient,
        reduce_gradient,
        vectors[5],
    )


def solution(mesh):
    depth = mesh.shape["dp"] // 4
    fine = Mesh(mesh.devices.reshape(depth, 2, 2, 2), ALL)
    dp = ("z", "y", "x")
    placed = (
        P(dp, None),
        P(),
        P(),
        P(dp, None, "c"),
        P(dp, "c"),
        P(),
        P(),
        P(),
        P(dp, "c"),
        P("c"),
        P(dp, "c"),
        P(),
        P(dp),
        P(dp),
        P(dp, None),
        P(dp, None),
    )
    return jax.shard_map(
        functools.partial(body, depth),
        mesh=fine,
        in_specs=placed,
        out_specs=(
            P(dp, None),
            P(dp, None),
            P(dp),
            P(dp),
            P(dp, None, "c"),
            P(dp, "c"),
            P(dp),
            P(dp),
            P(dp),
            P(dp, "c"),
            P("c", dp),
            P(dp, "c"),
            P(dp),
        ),
        check_vma=False,
    )
```

```python
import functools

import jax
import jax.numpy as jnp
from jax import lax
from jax.experimental import pallas as pl
from jax.experimental.pallas import tpu as pltpu
from jax.sharding import Mesh
from jax.sharding import PartitionSpec as P

HEAD = 128
WINDOW = 256
CHUNK = 128
SCALE = HEAD**-0.5
ALL = ("z", "y", "x", "c")
BF = jnp.bfloat16
F32 = jnp.float32
ACROSS = (((1,), (1,)), ((), ()))
ROWS = (((0,), (0,)), ((), ()))
PLAIN = (((1,), (0,)), ((), ()))


def dot(a, b, dims=PLAIN):
    return lax.dot_general(a, b, dims, preferred_element_type=F32)


def pairs_of(depth, route):
    def flat(z, y, x, c):
        return ((z * 2 + y) * 2 + x) * 2 + c

    found = []
    for z in range(depth):
        for y in range(2):
            for x in range(2):
                for c in range(2):
                    goal = route(y, x, c)
                    if goal is not None:
                        found.append((flat(z, y, x, c), flat(z, *goal)))
    return found


def bounds_of(group_sizes, prefix_lengths, solution_lengths, row_count):
    entries = solution_lengths.shape[1]
    position = jnp.arange(entries, dtype=jnp.int32)
    counted = jnp.where(position[None, :] < group_sizes[:, None], solution_lengths, 0)
    pieces = jnp.concatenate([prefix_lengths[:, None], counted], axis=1)
    flat = pieces.reshape(-1)
    count = flat.shape[0]
    index = jnp.arange(count, dtype=jnp.int32)
    ends = jnp.sum(jnp.where(index[None, :] <= index[:, None], flat[None, :], 0), axis=1)
    slot = jnp.arange(row_count, dtype=jnp.int32)
    passed = slot[:, None] >= ends[None, :]
    piece_start = jnp.max(jnp.where(passed, ends[None, :], 0), axis=1)
    group_end = ends.reshape(pieces.shape)[:, -1]
    over = slot[:, None] >= group_end[None, :]
    group_start = jnp.max(jnp.where(over, group_end[None, :], 0), axis=1)
    group_index = jnp.sum(over.astype(jnp.int32), axis=1)
    member = group_index[:, None] == jnp.arange(pieces.shape[0], dtype=jnp.int32)[None, :]
    prefix_end = group_start + jnp.sum(jnp.where(member, prefix_lengths[None, :], 0), axis=1)
    live = slot < ends[-1]
    piece_start = jnp.where(live, piece_start, slot)
    group_start = jnp.where(live, group_start, slot)
    prefix_end = jnp.where(live, prefix_end, slot)
    return jnp.stack([group_start, prefix_end, piece_start], axis=1), live


def key_range(i):
    return max(0, i * CHUNK - WINDOW), (i + 1) * CHUNK


def allowed_tile(info, i, lo, hi):
    rows = info[i * CHUNK : (i + 1) * CHUNK, :]
    start, stop, piece = rows[:, 0:1], rows[:, 1:2], rows[:, 2:3]
    s = lax.broadcasted_iota(jnp.int32, (CHUNK, hi - lo), 0) + i * CHUNK
    t = lax.broadcasted_iota(jnp.int32, (CHUNK, hi - lo), 1) + lo
    return (t <= s) & ((t >= piece) | ((t >= start) & (t < stop)))


def tiles_of(p_ref, width):
    found = []
    for i in range(p_ref.shape[0] // CHUNK):
        lo, hi = key_range(i)
        rows = slice(i * CHUNK, (i + 1) * CHUNK)
        for h in range(width // HEAD):
            qs, ks, vs = (slice(c * width + h * HEAD, c * width + (h + 1) * HEAD) for c in range(3))
            found.append((i, rows, slice(lo, hi), qs, ks, vs))
    return found


def masks_of(info_ref, block):
    info = info_ref[...]
    return [allowed_tile(info, i, *key_range(i)) for i in range(block // CHUNK)]


def attend_kernel(info_ref, p_ref, o_ref, l_ref):
    block, width = p_ref.shape
    width = width // 3
    masks = masks_of(info_ref, block)
    tiles = tiles_of(p_ref, width)
    raw = [dot(p_ref[rows, qs], p_ref[keys, ks], ACROSS) for _, rows, keys, qs, ks, _ in tiles]
    low = []
    for (i, rows, _, qs, _, _), score in zip(tiles, raw):
        scores = jnp.where(masks[i], score * SCALE, -1e30)
        peak = jnp.max(scores, axis=-1, keepdims=True)
        e = jnp.exp(scores - peak)
        total = jnp.sum(e, axis=-1, keepdims=True)
        low.append((e * (1.0 / total)).astype(BF))
        l_ref[rows, qs] = jnp.broadcast_to(peak + jnp.log(total), (CHUNK, HEAD))
    for (_, rows, keys, qs, _, vs), soft in zip(tiles, low):
        o_ref[rows, qs] = dot(soft, p_ref[keys, vs]).astype(BF)


def attend_back_kernel(info_ref, p_ref, g_ref, l_ref, d_ref, dk_ref, dv_ref):
    block, width = p_ref.shape
    width = width // 3
    masks = masks_of(info_ref, block)
    tiles = tiles_of(p_ref, width)
    dk_ref[...] = jnp.zeros_like(dk_ref)
    dv_ref[...] = jnp.zeros_like(dv_ref)
    raw = [dot(p_ref[rows, qs], p_ref[keys, ks], ACROSS) for _, rows, keys, qs, ks, _ in tiles]
    tangents = [dot(g_ref[rows, qs], p_ref[keys, vs], ACROSS) for _, rows, keys, qs, _, vs in tiles]
    kept = []
    for (i, rows, _, qs, _, _), score, tangent in zip(tiles, raw, tangents):
        scores = jnp.where(masks[i], score * SCALE, -1e30)
        soft = jnp.exp(scores - l_ref[rows, qs.start : qs.start + 1])
        back = soft * tangent
        low = (back - soft * jnp.sum(back, axis=-1, keepdims=True)).astype(BF)
        kept.append((soft.astype(BF), low))
    for (_, rows, keys, qs, ks, _), (soft, low) in zip(tiles, kept):
        d_ref[rows, qs] = (dot(low, p_ref[keys, ks]) * SCALE).astype(BF)
        dk_ref[keys, qs] += dot(low, p_ref[rows, qs], ROWS)
        dv_ref[keys, qs] += dot(soft, g_ref[rows, qs], ROWS)
    d_ref[:, width : 2 * width] = (dk_ref[...] * SCALE).astype(BF)
    d_ref[:, 2 * width :] = dv_ref[...].astype(BF)


def params(mib=48):
    return pltpu.CompilerParams(vmem_limit_bytes=mib << 20)


def cost(flops, moved, exps=0):
    return pl.CostEstimate(flops=flops, bytes_accessed=moved, transcendentals=exps)


def attend(info, projected, block):
    sides, rows, width = projected.shape
    spec = lambda n: pl.BlockSpec((None, block, n), lambda b, c: (c, b, 0))
    return pl.pallas_call(
        attend_kernel,
        grid=(rows // block, sides),
        in_specs=[pl.BlockSpec((block, info.shape[1]), lambda b, c: (b, 0)), spec(width)],
        out_specs=[spec(width // 3)] * 2,
        out_shape=[jax.ShapeDtypeStruct((sides, rows, width // 3), t) for t in (BF, F32)],
        compiler_params=params(),
        cost_estimate=cost(16 * rows * block * width, 8 * rows * width * 2, rows * block * 4),
        name="attend",
    )(info, projected)


def attend_back(info, projected, mixed_back, log_sums, block):
    sides, rows, width = projected.shape
    spec = lambda n: pl.BlockSpec((None, block, n), lambda b, c: (c, b, 0))
    return pl.pallas_call(
        attend_back_kernel,
        grid=(rows // block, sides),
        in_specs=[pl.BlockSpec((block, info.shape[1]), lambda b, c: (b, 0)), spec(width), spec(width // 3), spec(width // 3)],
        out_specs=spec(width),
        out_shape=jax.ShapeDtypeStruct((sides, rows, width), BF),
        scratch_shapes=[pltpu.VMEM((block, width // 3), F32)] * 2,
        compiler_params=params(),
        cost_estimate=cost(40 * rows * block * width, 16 * rows * width * 2, rows * block * 4),
        name="attend_back",
    )(info, projected, mixed_back, log_sums)


def steps(width, step=256):
    return [slice(j, min(j + step, width)) for j in range(0, width, step)]


def project_kernel(a_ref, w_ref, o_ref):
    for s in steps(w_ref.shape[1]):
        o_ref[:, s] = dot(a_ref[...], w_ref[:, s]).astype(BF)


def project(rows, weights, width, column):
    m, k = rows.shape
    sides = weights.shape[0]
    return pl.pallas_call(
        project_kernel,
        grid=(sides,),
        in_specs=[pl.BlockSpec((m, k), lambda c: (0, 0)), pl.BlockSpec((None, k, width), lambda c: (c, 0, column))],
        out_specs=pl.BlockSpec((None, m, width), lambda c: (c, 0, 0)),
        out_shape=jax.ShapeDtypeStruct((sides, m, width), BF),
        compiler_params=params(),
        cost_estimate=cost(2 * sides * m * k * width, 2 * (m * k + sides * k * width + sides * m * width)),
        name="project",
    )(rows, weights)


def expand_kernel(a_ref, w_ref, b_ref, o_ref, d_ref):
    root, cubic = 0.7978845608028654, 0.044715
    for s in steps(w_ref.shape[1]):
        v = dot(a_ref[...], w_ref[:, s]) + b_ref[:, s]
        square = v * v
        t = jnp.tanh(v * (root + root * cubic * square))
        half = 0.5 + 0.5 * t
        o_ref[:, s] = (v * half).astype(BF)
        d_ref[:, s] = half + v * (half * (1.0 - t)) * (root + 3.0 * root * cubic * square)


def expand(rows, weights, bias):
    m, k = rows.shape
    sides, _, n = weights.shape
    tile = min(n, 256)
    out = pl.BlockSpec((None, m, tile), lambda c, j: (c, 0, j))
    return pl.pallas_call(
        expand_kernel,
        grid=(sides, n // tile),
        in_specs=[
            pl.BlockSpec((m, k), lambda c, j: (0, 0)),
            pl.BlockSpec((None, k, tile), lambda c, j: (c, 0, j)),
            pl.BlockSpec((None, 1, tile), lambda c, j: (c, 0, j)),
        ],
        out_specs=[out, out],
        out_shape=[jax.ShapeDtypeStruct((sides, m, n), BF), jax.ShapeDtypeStruct((sides, m, n), F32)],
        compiler_params=params(),
        cost_estimate=cost(2 * sides * m * k * n, 2 * (m * k + sides * k * n) + 6 * sides * m * n, sides * m * n),
        name="expand",
    )(rows, weights, bias)


def expand_back_kernel(a_ref, w_ref, d_ref, o_ref, s_ref):
    for s in steps(w_ref.shape[1]):
        back = dot(a_ref[...], w_ref[:, s]) * d_ref[:, s]
        o_ref[:, s] = back.astype(BF)
        s_ref[:, s] = jnp.sum(back, axis=0, keepdims=True)


def expand_back(rows, weights, slope):
    m, k = rows.shape
    sides, _, n = weights.shape
    tile = min(n, 512)
    out = pl.BlockSpec((None, m, tile), lambda c, j: (c, 0, j))
    return pl.pallas_call(
        expand_back_kernel,
        grid=(sides, n // tile),
        in_specs=[
            pl.BlockSpec((m, k), lambda c, j: (0, 0)),
            pl.BlockSpec((None, k, tile), lambda c, j: (c, 0, j)),
            out,
        ],
        out_specs=[out, pl.BlockSpec((None, 1, tile), lambda c, j: (c, 0, j))],
        out_shape=[jax.ShapeDtypeStruct((sides, m, n), BF), jax.ShapeDtypeStruct((sides, 1, n), F32)],
        compiler_params=params(),
        cost_estimate=cost(2 * sides * m * k * n, 2 * (m * k + sides * k * n) + 6 * sides * m * n),
        name="expand_back",
    )(rows, weights, slope)


def contract_kernel(a_ref, w_ref, top_ref, low_ref):
    half = top_ref.shape[0]
    for s in steps(w_ref.shape[1]):
        total = dot(a_ref[0], w_ref[0, s, :], ACROSS)
        for c in range(1, a_ref.shape[0]):
            total = total + dot(a_ref[c], w_ref[c, s, :], ACROSS)
        top_ref[:, s] = total[:half].astype(BF)
        low_ref[:, s] = total[half:].astype(BF)


def contract(terms, weights, column, side):
    sides, m, n = terms.shape
    d = weights.shape[1]
    m = m // 2
    tile = min(d, 512)
    half = pl.BlockSpec((m // 2, tile), lambda j: (0, j))
    out = jax.ShapeDtypeStruct((m // 2, d), BF)
    return pl.pallas_call(
        contract_kernel,
        grid=(d // tile,),
        in_specs=[
            pl.BlockSpec((sides, m, n), lambda j: (0, side, 0)),
            pl.BlockSpec((sides, tile, n), lambda j: (0, j, column)),
        ],
        out_specs=[half, half],
        out_shape=[out, out],
        compiler_params=params(),
        cost_estimate=cost(2 * sides * m * n * d, 2 * (sides * m * n + sides * n * d + m * d)),
        name="contract",
    )(terms, weights)


def outer_kernel(pairs, adds, pick_ref, *refs):
    o_ref = refs[-1]
    start = 0
    for i in range(pairs):
        a_ref, r_ref = refs[2 * i], refs[2 * i + 1]
        for s in steps(r_ref.shape[1]):
            place = slice(start + s.start, start + s.stop)
            total = dot(a_ref[...], r_ref[:, s], ROWS)
            if adds:
                total = total + refs[2 * pairs][:, place].astype(F32)
            o_ref[:, place] = total.astype(BF)
        start += r_ref.shape[1]


def outer(pick, pairs, depth, extra=None):
    m, d = pairs[0][0].shape
    sides = pick.shape[0]
    total = sum(r.shape[2] for _, r in pairs)
    tile = d // depth
    place = pl.BlockSpec((None, None, tile, total), lambda c, i, s: (i, c, 0, 0))
    specs, args = [], []
    for a, r in pairs:
        specs.append(pl.BlockSpec((m, tile), lambda c, i, s: (0, i)))
        specs.append(pl.BlockSpec((None, m, r.shape[2]), lambda c, i, s: (s[c], 0, 0)))
        args += [a, r]
    if extra is not None:
        specs.append(place)
        args.append(extra)
    return pl.pallas_call(
        functools.partial(outer_kernel, len(pairs), extra is not None),
        grid_spec=pltpu.PrefetchScalarGridSpec(
            num_scalar_prefetch=1, grid=(sides, depth), in_specs=specs, out_specs=place
        ),
        out_shape=jax.ShapeDtypeStruct((depth, sides, tile, total), BF),
        compiler_params=params(),
        cost_estimate=cost(2 * sides * m * d * total, 2 * (m * d + sides * m * total + sides * d * total)),
        name="outer",
    )(pick, *args)


TILE = 128


def whole(v):
    return pl.BlockSpec((TILE, v.shape[1]), lambda i: (i, 0))


def vector(v):
    return pl.BlockSpec(v.shape, lambda i: (0, 0))


def halves(v):
    count = v.shape[0] // TILE
    return (
        pl.BlockSpec((TILE, v.shape[1]), lambda i: (jnp.minimum(i, count - 1), 0)),
        pl.BlockSpec((TILE, v.shape[1]), lambda i: (jnp.maximum(i - count, 0), 0)),
    )


def in_half(count, use):
    for side in range(2):
        pl.when(pl.program_id(0) // count == side)(functools.partial(use, side))


def total_of(terms, side):
    picked = [t[...].astype(F32) for t in terms[3 * side : 3 * side + 3]]
    return picked[0] + picked[1] + picked[2]


def unit(values):
    center = values - jnp.mean(values, axis=-1, keepdims=True)
    factor = lax.rsqrt(jnp.mean(center * center, axis=-1, keepdims=True) + 1e-05)
    return center * factor, factor


def unit_back(tangent, gain, xhat, factor):
    e = tangent * gain
    return factor * (
        e - jnp.mean(e, axis=-1, keepdims=True) - xhat * jnp.mean(e * xhat, axis=-1, keepdims=True)
    )


def add_sums(s_ref, rows):
    sums = jnp.concatenate([jnp.sum(r, axis=0, keepdims=True) for r in rows], axis=0)
    first = pl.program_id(0) == 0

    @pl.when(first)
    def _():
        s_ref[0 : len(rows), :] = sums

    @pl.when(jnp.logical_not(first))
    def _():
        s_ref[0 : len(rows), :] += sums


def first_kernel(count, x_ref, gain_ref, shift_ref, *outs):
    def use(side):
        xhat, _ = unit(x_ref[...].astype(F32))
        outs[side][...] = (xhat * gain_ref[...] + shift_ref[...]).astype(BF)

    in_half(count, use)


def middle_kernel(count, *refs):
    terms, (x_ref, bias_ref, gain_ref, shift_ref, m_ref), outs = refs[:6], refs[6:11], refs[11:]

    def use(side):
        middle = x_ref[...].astype(F32) + total_of(terms, side) + bias_ref[...]
        m_ref[...] = middle
        xhat, _ = unit(middle)
        outs[side][...] = (xhat * gain_ref[...] + shift_ref[...]).astype(BF)

    in_half(count, use)


def output_kernel(count, *refs):
    terms, (m_ref, live_ref, bias_ref, o_ref) = refs[:6], refs[6:]

    def use(side):
        o_ref[...] = (live_ref[:, 0:1] * (m_ref[...] + total_of(terms, side) + bias_ref[...])).astype(BF)

    in_half(count, use)


def middle_back_kernel(count, *refs):
    terms, (m_ref, g_ref, live_ref, gain_ref, b_ref, s_ref), outs = refs[:6], refs[6:12], refs[12:]

    def use(side):
        tangent = total_of(terms, side)
        xhat, factor = unit(m_ref[...])
        upstream = live_ref[:, 0:1] * g_ref[...].astype(F32)
        back = upstream + unit_back(tangent, gain_ref[...], xhat, factor)
        b_ref[...] = back
        outs[side][...] = back.astype(BF)
        add_sums(s_ref, [tangent * xhat, tangent, back, upstream])

    in_half(count, use)


def input_back_kernel(count, *refs):
    terms, (x_ref, b_ref, gain_ref, o_ref, s_ref) = refs[:6], refs[6:]

    def use(side):
        tangent = total_of(terms, side)
        xhat, factor = unit(x_ref[...].astype(F32))
        o_ref[...] = (b_ref[...] + unit_back(tangent, gain_ref[...], xhat, factor)).astype(BF)
        add_sums(s_ref, [tangent * xhat, tangent])

    in_half(count, use)


def over_rows(kernel, terms, rows, vectors, wholes=(), pieces=0, sums=False):
    m = rows[0].shape[0]
    d = rows[0].shape[1]
    half = jax.ShapeDtypeStruct((m // 2, d), BF)
    upper, lower = halves(half)
    specs = [upper] * 3 + [lower] * 3 if terms else []
    specs += [whole(r) for r in rows] + [vector(v) for v in vectors]
    outs = [jax.ShapeDtypeStruct((m, d), t) for t in wholes]
    out_specs = [whole(o) for o in outs]
    if sums:
        outs.append(jax.ShapeDtypeStruct((8, d), F32))
        out_specs.append(vector(outs[-1]))
    outs += [half] * pieces
    out_specs += [upper, lower][:pieces]
    return pl.pallas_call(
        functools.partial(kernel, m // 2 // TILE),
        grid=(m // TILE,),
        in_specs=specs,
        out_specs=out_specs,
        out_shape=outs,
        compiler_params=params(),
        cost_estimate=cost(20 * m * d, 16 * m * d),
        name=kernel.__name__.replace("_kernel", ""),
    )(*terms, *rows, *vectors)


def assemble_kernel(own_ref, *refs):
    pieces, o_ref, sems = refs[:8], refs[8], refs[9]
    rows = pieces[0].shape[0]
    for side in range(2):

        @pl.when(own_ref[0] == 1 - side)
        def _():
            copies = [
                pltpu.make_async_copy(pieces[4 * side + k], o_ref.at[pl.ds(k * rows, rows), :], sems.at[k])
                for k in range(4)
            ]
            for c in copies:
                c.start()
            for c in copies:
                c.wait()


def assemble(own, mine, theirs):
    rows, d = mine[0].shape
    anywhere = pl.BlockSpec(memory_space=pl.ANY)
    return pl.pallas_call(
        assemble_kernel,
        in_specs=[pl.BlockSpec(memory_space=pltpu.SMEM)] + [anywhere] * 8,
        out_specs=pl.BlockSpec(memory_space=pltpu.VMEM),
        out_shape=jax.ShapeDtypeStruct((4 * rows, d), BF),
        scratch_shapes=[pltpu.SemaphoreType.DMA((4,))],
        compiler_params=params(16),
        cost_estimate=cost(0, 16 * rows * d),
        name="assemble",
    )(own, *mine, *theirs)


def place_kernel(plane_ref, *refs):
    for k in range(4):

        @pl.when(pl.program_id(0) == k)
        def _():
            start = 0
            for o_ref in refs[4:]:
                if len(o_ref.shape) == 3:
                    width = o_ref.shape[2]
                    for j in range(o_ref.shape[0]):
                        o_ref[j] = refs[k][:, start : start + width].astype(o_ref.dtype)
                        start += width
                else:
                    width = o_ref.shape[1]
                    o_ref[...] = refs[k][:, start : start + width].astype(o_ref.dtype)
                    start += width


def place(plane, pieces, axis, dtype, split=(1,)):
    m, n = pieces[0].shape
    unit_width = n // sum(split)
    outs, specs = [], []
    for count in split:
        if axis == 0:
            outs.append(jax.ShapeDtypeStruct((4 * m, n), dtype))
            specs.append(pl.BlockSpec((m, n), lambda k, p: (p[0] ^ k, 0)))
        elif count == 1:
            outs.append(jax.ShapeDtypeStruct((m, 4 * unit_width), dtype))
            specs.append(pl.BlockSpec((m, unit_width), lambda k, p: (0, p[0] ^ k)))
        else:
            outs.append(jax.ShapeDtypeStruct((count, m, 4 * unit_width), dtype))
            specs.append(pl.BlockSpec((count, m, unit_width), lambda k, p: (0, 0, p[0] ^ k)))
    return pl.pallas_call(
        place_kernel,
        grid_spec=pltpu.PrefetchScalarGridSpec(
            num_scalar_prefetch=1,
            grid=(4,),
            in_specs=[pl.BlockSpec((m, n), lambda k, p: (0, 0))] * 4,
            out_specs=specs,
        ),
        out_shape=outs,
        compiler_params=params(),
        cost_estimate=cost(0, 16 * m * n),
        name="place",
    )(plane, *pieces)


def part_kernel(plane_ref, v_ref, *outs):
    for k in range(4):

        @pl.when(pl.program_id(0) == k)
        def _():
            outs[k][...] = v_ref[...]


def part_rows(plane, v):
    m, n = v.shape[0] // 4, v.shape[1]
    return pl.pallas_call(
        part_kernel,
        grid_spec=pltpu.PrefetchScalarGridSpec(
            num_scalar_prefetch=1,
            grid=(4,),
            in_specs=[pl.BlockSpec((m, n), lambda k, p: (p[0] ^ k, 0))],
            out_specs=[pl.BlockSpec((m, n), lambda k, p: (0, 0))] * 4,
        ),
        out_shape=[jax.ShapeDtypeStruct((m, n), v.dtype)] * 4,
        compiler_params=params(),
        cost_estimate=cost(0, 16 * m * n),
        name="part_rows",
    )(plane, v)


def after(value, *others):
    return lax.optimization_barrier((value, *others))[0]


def body(
    depth,
    inputs,
    gamma_first,
    beta_first,
    heads_weight,
    output_weight,
    output_bias,
    gamma_second,
    beta_second,
    expand_weight,
    expand_bias,
    reduce_weight,
    reduce_bias,
    group_sizes,
    prefix_lengths,
    solution_lengths,
    cotangent,
):
    block, model = inputs.shape
    zi, yi, xi, ci = (lax.axis_index(a) for a in ALL)
    plane = yi * 2 + xi
    own = xi == ci
    send = lambda v, route: lax.ppermute(v, ALL, pairs_of(depth, route))
    wide = lambda v: v.astype(F32)

    def near_of(v):
        return send(v, lambda y, x, c: (y, x, c) if c == x else (y, 1 - x, 1 - c))

    def far_of(v):
        return send(v, lambda y, x, c: (1 - y, x, c) if c == x else (1 - y, 1 - x, 1 - c))

    flip_y = lambda y, x, c: (1 - y, x, c)
    owners_y = lambda y, x, c: (1 - y, x, c) if c == x else None
    others_y = lambda y, x, c: (1 - y, x, c) if c != x else None
    owners_x = lambda y, x, c: (y, 1 - x, c) if c == x else None
    others_x = lambda y, x, c: (y, 1 - x, c) if c != x else None

    def spread_out(top, low):
        y_low, x_top = send(low, owners_y), send(top, owners_x)
        return top, low, send(top, owners_y), y_low, x_top, send(low, owners_x)

    def spread_on(moved):
        top, low, y_top, y_low, x_top, x_low = moved
        far_low, far_top = send(y_low, owners_x), send(x_top, others_y)
        return assemble(own_flag, (top, low, y_top, y_low), (x_top, x_low, far_top, far_low))

    def collect(far, near):
        far_top, far_low = far
        near_top, near_low = near
        by_y, to_far = send(far_top, flip_y), send(far_low, others_x)
        by_x = send(near_low, others_x)
        from_y = send((wide(far_low) + wide(to_far)).astype(BF), owners_y)
        from_x = send((wide(near_top) + wide(by_y)).astype(BF), others_x)
        return (near_top, from_x, by_y, near_low, by_x, from_y), (to_far, by_y)

    def from_owner(v):
        return jnp.where(own, v, send(v, lambda y, x, c: (y, x, 1 - c) if c == x else None))

    def shuffle(pieces, *first):
        routes = (
            lambda y, x, c: (y, 1 - x, c),
            lambda y, x, c: (1 - y, x, c),
            lambda y, x, c: (1 - y, 1 - x, c),
        )
        pieces = lax.optimization_barrier((*pieces, *first))[:4]
        return [pieces[0]] + [send(pieces[k], routes[k - 1]) for k in (1, 2, 3)]

    def columns(v, k):
        width = v.shape[-1] // 4
        return lax.dynamic_slice_in_dim(v, (plane ^ k) * width, width, axis=-1)

    def gather(pieces):
        full = lax.all_gather(place(plane_flag, pieces, 0, BF)[0], ("c", "z"), axis=0, tiled=True)
        return full.reshape(2, full.shape[0] // 2, full.shape[1])

    def scatter(terms, axes):
        return lax.psum_scatter(terms.reshape(-1, terms.shape[-1]), axes, scatter_dimension=0, tiled=True)

    pick = ci.astype(jnp.int32).reshape(1)
    plane_flag = plane.astype(jnp.int32).reshape(1)
    own_flag = own.astype(jnp.int32).reshape(1)
    row = lambda v: wide(v).reshape(1, -1)
    shard, _, local = heads_weight.shape
    part = local // 4
    inner = expand_weight.shape[1] // 4

    def attention_columns(k):
        heads = columns(heads_weight, k)
        return jnp.concatenate([heads[:, 0], heads[:, 1], heads[:, 2], columns(output_weight, k)], axis=1)

    heads_got = shuffle([attention_columns(k) for k in range(4)])
    heads_all = gather(heads_got)

    info, live = bounds_of(group_sizes, prefix_lengths, solution_lengths, block)
    info = jnp.pad(info, ((0, 0), (0, 5)))
    live_mask = wide(live)[:, None]
    live_wide = jnp.broadcast_to(live_mask, (block, 128))
    info_two = jnp.concatenate([near_of(info), far_of(info)], axis=0)
    first_own = over_rows(first_kernel, (), (inputs,), (row(gamma_first), row(beta_first)), pieces=2)
    first_own = lax.optimization_barrier((*first_own, *heads_got))[:2]
    first = spread_on(spread_out(*first_own))

    expand_got = shuffle([columns(expand_weight, k) for k in range(4)], first)
    expand_all = gather(expand_got)
    reduce_got = shuffle([columns(reduce_weight, k) for k in range(4)], *expand_got)
    reduce_all = gather(reduce_got)
    bias_mine = lax.dynamic_slice_in_dim(expand_bias, plane * inner, inner).reshape(1, 1, inner)
    bias_other = send(bias_mine, lambda y, x, c: (y, x, 1 - c))
    bias = wide(
        jnp.where(ci == 0, jnp.concatenate([bias_mine, bias_other]), jnp.concatenate([bias_other, bias_mine]))
    )
    upstream_own = (live_mask * wide(cotangent)).astype(BF)
    upstream_own = (upstream_own[: block // 2], upstream_own[block // 2 :])
    upstream_moved = spread_out(*lax.optimization_barrier((*upstream_own, *reduce_got))[:2])

    both = jnp.arange(2, dtype=jnp.int32)
    projected = project(first, heads_all, 3 * part, 0)
    mixed, log_sums = attend(info_two, projected, block)
    far = contract(mixed, heads_all, 3, 1)
    mixed_near, *upstream_moved = lax.optimization_barrier((mixed, *upstream_moved, *far))[:7]
    attended, _ = collect(far, contract(mixed_near, heads_all, 3, 0))
    middle, *second_own = over_rows(
        middle_kernel, attended, (inputs,), (row(output_bias), row(gamma_second), row(beta_second)), (F32,), pieces=2
    )
    second = spread_on(spread_out(*second_own))
    upstream_low = spread_on(lax.optimization_barrier((*upstream_moved, second))[:6])
    activated, slope = expand(second, expand_all, bias)
    reduce_terms = outer(both, [(upstream_low, activated)], depth)
    reduce_part = scatter(reduce_terms, ("z", "c"))

    slope, upstream_last, _ = lax.optimization_barrier((slope, upstream_low, reduce_terms))
    sum_low, expand_bias_gradient = expand_back(upstream_last, reduce_all, slope)
    expand_bias_gradient = expand_bias_gradient.reshape(2, inner)
    far, near = contract(sum_low, expand_all, 0, 1), contract(sum_low, expand_all, 0, 0)
    second_back, moved = collect(far, near)
    expand_terms = outer(both, [(second, after(sum_low, *moved, *near))], depth)
    expand_part = scatter(expand_terms, ("z", "c"))
    second_back = lax.optimization_barrier((*second_back, expand_terms))[:6]
    middle_back, sums_second, *middle_own = over_rows(
        middle_back_kernel,
        second_back,
        (middle, cotangent, live_wide),
        (row(gamma_second),),
        (F32,),
        pieces=2,
        sums=True,
    )
    active_last = after(activated, *middle_own)
    far, near = contract(active_last, reduce_all, 0, 1), contract(active_last, reduce_all, 0, 0)
    branch, moved = collect(far, near)
    middle_low = spread_on(spread_out(*middle_own))

    mixed_back = project(after(middle_low, reduce_part, *far, *near), heads_all, part, 3)
    projected_back = attend_back(info_two, projected, after(mixed_back, moved[0]), log_sums, block)
    projected_back = after(projected_back, moved[1])
    heads_terms = outer(both, [(first, projected_back), (middle_low, mixed)], depth)
    heads_part = scatter(after(heads_terms, expand_part), ("z", "c"))
    far = contract(after(projected_back, heads_terms), heads_all, 0, 1)
    reduce_got = shuffle(part_rows(plane_flag, reduce_part))
    projected_near, *rest = lax.optimization_barrier((projected_back, *branch, *reduce_got, *far))
    branch, reduce_got = rest[:6], rest[6:10]
    near = contract(projected_near, heads_all, 0, 0)
    first_back, _ = collect(far, near)
    (outputs,) = over_rows(output_kernel, branch, (middle, live_wide), (row(reduce_bias),), (BF,))
    outputs = from_owner(outputs)
    (reduce_gradient,) = place(plane_flag, reduce_got, 1, F32)
    *first_back, outputs, reduce_gradient = lax.optimization_barrier((*first_back, outputs, reduce_gradient))
    input_gradient, sums_first = over_rows(
        input_back_kernel, first_back, (inputs, middle_back), (row(gamma_first),), (BF,), sums=True
    )
    input_gradient = from_owner(input_gradient)

    expand_got = shuffle(part_rows(plane_flag, expand_part), *first_back)
    (expand_gradient,) = place(plane_flag, expand_got, 1, F32)
    gamma_first_gradient, beta_first_gradient = sums_first[0], sums_first[1]
    gamma_second_gradient, beta_second_gradient = sums_second[0], sums_second[1]
    output_bias_gradient, reduce_bias_gradient = sums_second[2], sums_second[3]

    vectors = jnp.stack(
        [
            gamma_first_gradient,
            beta_first_gradient,
            output_bias_gradient,
            gamma_second_gradient,
            beta_second_gradient,
            reduce_bias_gradient,
        ]
    )
    vectors = jnp.where(own, vectors, 0.0)
    placed = lax.dynamic_update_slice(jnp.zeros((2, 4 * inner), F32), expand_bias_gradient, (0, plane * inner))
    sums = jnp.concatenate([vectors.reshape(-1), placed.reshape(-1)]).reshape(-1, 128)
    for route in (
        lambda y, x, c: (y, x, 1 - c),
        lambda y, x, c: (y, 1 - x, c),
        lambda y, x, c: (1 - y, x, c),
    ):
        sums = sums + send(sums, route)
    sums, expand_gradient = lax.optimization_barrier((sums, expand_gradient))
    step = 1
    while step < depth:
        sums = sums + lax.ppermute(sums, "z", [(i, i ^ step) for i in range(depth)])
        step *= 2
    flat = sums.reshape(-1)
    index = zi * 4 + plane
    vectors = lax.dynamic_slice_in_dim(flat[: 6 * model].reshape(6, model), index * shard, shard, axis=1)
    placed = flat[6 * model :].reshape(2, 4 * inner)
    count = 4 * inner // (4 * depth)
    expand_bias_gradient = lax.dynamic_slice(placed, (ci, index * count), (1, count))
    heads_part, reduce_gradient, expand_gradient, outputs, input_gradient, vectors, expand_bias_gradient = (
        lax.optimization_barrier(
            (heads_part, reduce_gradient, expand_gradient, outputs, input_gradient, vectors, expand_bias_gradient)
        )
    )
    heads_got = shuffle(part_rows(plane_flag, heads_part))
    heads_gradient, output_gradient = place(plane_flag, heads_got, 1, F32, (3, 1))
    heads_gradient = heads_gradient.transpose(1, 0, 2)
    return (
        outputs,
        input_gradient,
        vectors[0],
        vectors[1],
        heads_gradient,
        output_gradient,
        vectors[2],
        vectors[3],
        vectors[4],
        expand_gradient,
        expand_bias_gradient,
        reduce_gradient,
        vectors[5],
    )


def solution(mesh):
    depth = mesh.shape["dp"] // 4
    fine = Mesh(mesh.devices.reshape(depth, 2, 2, 2), ALL)
    dp = ("z", "y", "x")
    placed = (
        P(dp, None),
        P(),
        P(),
        P(dp, None, "c"),
        P(dp, "c"),
        P(),
        P(),
        P(),
        P(dp, "c"),
        P("c"),
        P(dp, "c"),
        P(),
        P(dp),
        P(dp),
        P(dp, None),
        P(dp, None),
    )
    return jax.shard_map(
        functools.partial(body, depth),
        mesh=fine,
        in_specs=placed,
        out_specs=(
            P(dp, None),
            P(dp, None),
            P(dp),
            P(dp),
            P(dp, None, "c"),
            P(dp, "c"),
            P(dp),
            P(dp),
            P(dp),
            P(dp, "c"),
            P("c", dp),
            P(dp, "c"),
            P(dp),
        ),
        check_vma=False,
    )
```

```python
import functools

import jax
import jax.numpy as jnp
from jax import lax
from jax.experimental import pallas as pl
from jax.experimental.pallas import tpu as pltpu
from jax.sharding import Mesh
from jax.sharding import PartitionSpec as P

HEAD = 128
WINDOW = 256
CHUNK = 128
SCALE = HEAD**-0.5
ALL = ("z", "y", "x", "c")
BF = jnp.bfloat16
F32 = jnp.float32
ACROSS = (((1,), (1,)), ((), ()))
ROWS = (((0,), (0,)), ((), ()))
PLAIN = (((1,), (0,)), ((), ()))


def dot(a, b, dims=PLAIN):
    return lax.dot_general(a, b, dims, preferred_element_type=F32)


def pairs_of(depth, route):
    def flat(z, y, x, c):
        return ((z * 2 + y) * 2 + x) * 2 + c

    found = []
    for z in range(depth):
        for y in range(2):
            for x in range(2):
                for c in range(2):
                    goal = route(y, x, c)
                    if goal is not None:
                        found.append((flat(z, y, x, c), flat(z, *goal)))
    return found


def bounds_of(group_sizes, prefix_lengths, solution_lengths, row_count):
    entries = solution_lengths.shape[1]
    position = jnp.arange(entries, dtype=jnp.int32)
    counted = jnp.where(position[None, :] < group_sizes[:, None], solution_lengths, 0)
    pieces = jnp.concatenate([prefix_lengths[:, None], counted], axis=1)
    flat = pieces.reshape(-1)
    count = flat.shape[0]
    index = jnp.arange(count, dtype=jnp.int32)
    ends = jnp.sum(jnp.where(index[None, :] <= index[:, None], flat[None, :], 0), axis=1)
    slot = jnp.arange(row_count, dtype=jnp.int32)
    passed = slot[:, None] >= ends[None, :]
    piece_start = jnp.max(jnp.where(passed, ends[None, :], 0), axis=1)
    group_end = ends.reshape(pieces.shape)[:, -1]
    over = slot[:, None] >= group_end[None, :]
    group_start = jnp.max(jnp.where(over, group_end[None, :], 0), axis=1)
    group_index = jnp.sum(over.astype(jnp.int32), axis=1)
    member = group_index[:, None] == jnp.arange(pieces.shape[0], dtype=jnp.int32)[None, :]
    prefix_end = group_start + jnp.sum(jnp.where(member, prefix_lengths[None, :], 0), axis=1)
    live = slot < ends[-1]
    piece_start = jnp.where(live, piece_start, slot)
    group_start = jnp.where(live, group_start, slot)
    prefix_end = jnp.where(live, prefix_end, slot)
    return jnp.stack([group_start, prefix_end, piece_start], axis=1), live


def key_range(i):
    return max(0, i * CHUNK - WINDOW), (i + 1) * CHUNK


def allowed_tile(info, i, lo, hi):
    rows = info[i * CHUNK : (i + 1) * CHUNK, :]
    start, stop, piece = rows[:, 0:1], rows[:, 1:2], rows[:, 2:3]
    s = lax.broadcasted_iota(jnp.int32, (CHUNK, hi - lo), 0) + i * CHUNK
    t = lax.broadcasted_iota(jnp.int32, (CHUNK, hi - lo), 1) + lo
    return (t <= s) & ((t >= piece) | ((t >= start) & (t < stop)))


def tiles_of(p_ref, width):
    found = []
    for i in range(p_ref.shape[0] // CHUNK):
        lo, hi = key_range(i)
        rows = slice(i * CHUNK, (i + 1) * CHUNK)
        for h in range(width // HEAD):
            qs, ks, vs = (slice(c * width + h * HEAD, c * width + (h + 1) * HEAD) for c in range(3))
            found.append((i, rows, slice(lo, hi), qs, ks, vs))
    return found


def masks_of(info_ref, block):
    info = info_ref[...]
    return [allowed_tile(info, i, *key_range(i)) for i in range(block // CHUNK)]


def attend_kernel(info_ref, p_ref, o_ref, l_ref):
    block, width = p_ref.shape
    width = width // 3
    masks = masks_of(info_ref, block)
    tiles = tiles_of(p_ref, width)
    raw = [dot(p_ref[rows, qs], p_ref[keys, ks], ACROSS) for _, rows, keys, qs, ks, _ in tiles]
    low = []
    for (i, rows, _, qs, _, _), score in zip(tiles, raw):
        scores = jnp.where(masks[i], score * SCALE, -1e30)
        peak = jnp.max(scores, axis=-1, keepdims=True)
        e = jnp.exp(scores - peak)
        total = jnp.sum(e, axis=-1, keepdims=True)
        low.append((e * (1.0 / total)).astype(BF))
        l_ref[rows, qs] = jnp.broadcast_to(peak + jnp.log(total), (CHUNK, HEAD))
    for (_, rows, keys, qs, _, vs), soft in zip(tiles, low):
        o_ref[rows, qs] = dot(soft, p_ref[keys, vs]).astype(BF)


def attend_back_kernel(info_ref, p_ref, g_ref, l_ref, d_ref, dk_ref, dv_ref):
    block, width = p_ref.shape
    width = width // 3
    masks = masks_of(info_ref, block)
    tiles = tiles_of(p_ref, width)
    dk_ref[...] = jnp.zeros_like(dk_ref)
    dv_ref[...] = jnp.zeros_like(dv_ref)
    raw = [dot(p_ref[rows, qs], p_ref[keys, ks], ACROSS) for _, rows, keys, qs, ks, _ in tiles]
    tangents = [dot(g_ref[rows, qs], p_ref[keys, vs], ACROSS) for _, rows, keys, qs, _, vs in tiles]
    kept = []
    for (i, rows, _, qs, _, _), score, tangent in zip(tiles, raw, tangents):
        scores = jnp.where(masks[i], score * SCALE, -1e30)
        soft = jnp.exp(scores - l_ref[rows, qs.start : qs.start + 1])
        back = soft * tangent
        low = (back - soft * jnp.sum(back, axis=-1, keepdims=True)).astype(BF)
        kept.append((soft.astype(BF), low))
    for (_, rows, keys, qs, ks, _), (soft, low) in zip(tiles, kept):
        d_ref[rows, qs] = (dot(low, p_ref[keys, ks]) * SCALE).astype(BF)
        dk_ref[keys, qs] += dot(low, p_ref[rows, qs], ROWS)
        dv_ref[keys, qs] += dot(soft, g_ref[rows, qs], ROWS)
    d_ref[:, width : 2 * width] = (dk_ref[...] * SCALE).astype(BF)
    d_ref[:, 2 * width :] = dv_ref[...].astype(BF)


def params(mib=48):
    return pltpu.CompilerParams(vmem_limit_bytes=mib << 20)


def cost(flops, moved, exps=0):
    return pl.CostEstimate(flops=flops * 4, bytes_accessed=moved * 4, transcendentals=exps)


def attend(info, projected, block):
    sides, rows, width = projected.shape
    spec = lambda n: pl.BlockSpec((None, block, n), lambda b, c: (c, b, 0))
    return pl.pallas_call(
        attend_kernel,
        grid=(rows // block, sides),
        in_specs=[pl.BlockSpec((block, info.shape[1]), lambda b, c: (b, 0)), spec(width)],
        out_specs=[spec(width // 3)] * 2,
        out_shape=[jax.ShapeDtypeStruct((sides, rows, width // 3), t) for t in (BF, F32)],
        compiler_params=params(),
        cost_estimate=cost(16 * rows * block * width, 8 * rows * width * 2, rows * block * 4),
        name="attend",
    )(info, projected)


def attend_back(info, projected, mixed_back, log_sums, block):
    sides, rows, width = projected.shape
    spec = lambda n: pl.BlockSpec((None, block, n), lambda b, c: (c, b, 0))
    return pl.pallas_call(
        attend_back_kernel,
        grid=(rows // block, sides),
        in_specs=[pl.BlockSpec((block, info.shape[1]), lambda b, c: (b, 0)), spec(width), spec(width // 3), spec(width // 3)],
        out_specs=spec(width),
        out_shape=jax.ShapeDtypeStruct((sides, rows, width), BF),
        scratch_shapes=[pltpu.VMEM((block, width // 3), F32)] * 2,
        compiler_params=params(),
        cost_estimate=cost(40 * rows * block * width, 16 * rows * width * 2, rows * block * 4),
        name="attend_back",
    )(info, projected, mixed_back, log_sums)


def steps(width, step=256):
    return [slice(j, min(j + step, width)) for j in range(0, width, step)]


def project_kernel(a_ref, w_ref, o_ref):
    for s in steps(w_ref.shape[1]):
        o_ref[:, s] = dot(a_ref[...], w_ref[:, s]).astype(BF)


def project(rows, weights, width, column):
    m, k = rows.shape
    sides = weights.shape[0]
    return pl.pallas_call(
        project_kernel,
        grid=(sides,),
        in_specs=[pl.BlockSpec((m, k), lambda c: (0, 0)), pl.BlockSpec((None, k, width), lambda c: (c, 0, column))],
        out_specs=pl.BlockSpec((None, m, width), lambda c: (c, 0, 0)),
        out_shape=jax.ShapeDtypeStruct((sides, m, width), BF),
        compiler_params=params(),
        cost_estimate=cost(2 * sides * m * k * width, 2 * (m * k + sides * k * width + sides * m * width)),
        name="project",
    )(rows, weights)


def expand_kernel(a_ref, w_ref, b_ref, o_ref, d_ref):
    root, cubic = 0.7978845608028654, 0.044715
    for s in steps(w_ref.shape[1]):
        v = dot(a_ref[...], w_ref[:, s]) + b_ref[:, s]
        square = v * v
        t = jnp.tanh(v * (root + root * cubic * square))
        half = 0.5 + 0.5 * t
        o_ref[:, s] = (v * half).astype(BF)
        d_ref[:, s] = half + v * (half * (1.0 - t)) * (root + 3.0 * root * cubic * square)


def expand(rows, weights, bias):
    m, k = rows.shape
    sides, _, n = weights.shape
    tile = min(n, 256)
    out = pl.BlockSpec((None, m, tile), lambda c, j: (c, 0, j))
    return pl.pallas_call(
        expand_kernel,
        grid=(sides, n // tile),
        in_specs=[
            pl.BlockSpec((m, k), lambda c, j: (0, 0)),
            pl.BlockSpec((None, k, tile), lambda c, j: (c, 0, j)),
            pl.BlockSpec((None, 1, tile), lambda c, j: (c, 0, j)),
        ],
        out_specs=[out, out],
        out_shape=[jax.ShapeDtypeStruct((sides, m, n), BF), jax.ShapeDtypeStruct((sides, m, n), F32)],
        compiler_params=params(),
        cost_estimate=cost(2 * sides * m * k * n, 2 * (m * k + sides * k * n) + 6 * sides * m * n, sides * m * n),
        name="expand",
    )(rows, weights, bias)


def expand_back_kernel(a_ref, w_ref, d_ref, o_ref, s_ref):
    for s in steps(w_ref.shape[1]):
        back = dot(a_ref[...], w_ref[:, s]) * d_ref[:, s]
        o_ref[:, s] = back.astype(BF)
        s_ref[:, s] = jnp.sum(back, axis=0, keepdims=True)


def expand_back(rows, weights, slope):
    m, k = rows.shape
    sides, _, n = weights.shape
    tile = min(n, 512)
    out = pl.BlockSpec((None, m, tile), lambda c, j: (c, 0, j))
    return pl.pallas_call(
        expand_back_kernel,
        grid=(sides, n // tile),
        in_specs=[
            pl.BlockSpec((m, k), lambda c, j: (0, 0)),
            pl.BlockSpec((None, k, tile), lambda c, j: (c, 0, j)),
            out,
        ],
        out_specs=[out, pl.BlockSpec((None, 1, tile), lambda c, j: (c, 0, j))],
        out_shape=[jax.ShapeDtypeStruct((sides, m, n), BF), jax.ShapeDtypeStruct((sides, 1, n), F32)],
        compiler_params=params(),
        cost_estimate=cost(2 * sides * m * k * n, 2 * (m * k + sides * k * n) + 6 * sides * m * n),
        name="expand_back",
    )(rows, weights, slope)


def contract_kernel(a_ref, w_ref, top_ref, low_ref):
    half = top_ref.shape[0]
    for s in steps(w_ref.shape[1]):
        total = dot(a_ref[0], w_ref[0, s, :], ACROSS)
        for c in range(1, a_ref.shape[0]):
            total = total + dot(a_ref[c], w_ref[c, s, :], ACROSS)
        top_ref[:, s] = total[:half].astype(BF)
        low_ref[:, s] = total[half:].astype(BF)


def contract(terms, weights, column, side):
    sides, m, n = terms.shape
    d = weights.shape[1]
    m = m // 2
    tile = min(d, 512)
    half = pl.BlockSpec((m // 2, tile), lambda j: (0, j))
    out = jax.ShapeDtypeStruct((m // 2, d), BF)
    return pl.pallas_call(
        contract_kernel,
        grid=(d // tile,),
        in_specs=[
            pl.BlockSpec((sides, m, n), lambda j: (0, side, 0)),
            pl.BlockSpec((sides, tile, n), lambda j: (0, j, column)),
        ],
        out_specs=[half, half],
        out_shape=[out, out],
        compiler_params=params(),
        cost_estimate=cost(2 * sides * m * n * d, 2 * (sides * m * n + sides * n * d + m * d)),
        name="contract",
    )(terms, weights)


def outer_kernel(pairs, adds, pick_ref, *refs):
    o_ref = refs[-1]
    start = 0
    for i in range(pairs):
        a_ref, r_ref = refs[2 * i], refs[2 * i + 1]
        for s in steps(r_ref.shape[1]):
            place = slice(start + s.start, start + s.stop)
            total = dot(a_ref[...], r_ref[:, s], ROWS)
            if adds:
                total = total + refs[2 * pairs][:, place].astype(F32)
            o_ref[:, place] = total.astype(BF)
        start += r_ref.shape[1]


def outer(pick, pairs, depth, extra=None):
    m, d = pairs[0][0].shape
    sides = pick.shape[0]
    total = sum(r.shape[2] for _, r in pairs)
    tile = d // depth
    place = pl.BlockSpec((None, None, tile, total), lambda c, i, s: (i, c, 0, 0))
    specs, args = [], []
    for a, r in pairs:
        specs.append(pl.BlockSpec((m, tile), lambda c, i, s: (0, i)))
        specs.append(pl.BlockSpec((None, m, r.shape[2]), lambda c, i, s: (s[c], 0, 0)))
        args += [a, r]
    if extra is not None:
        specs.append(place)
        args.append(extra)
    return pl.pallas_call(
        functools.partial(outer_kernel, len(pairs), extra is not None),
        grid_spec=pltpu.PrefetchScalarGridSpec(
            num_scalar_prefetch=1, grid=(sides, depth), in_specs=specs, out_specs=place
        ),
        out_shape=jax.ShapeDtypeStruct((depth, sides, tile, total), BF),
        compiler_params=params(),
        cost_estimate=cost(2 * sides * m * d * total, 2 * (m * d + sides * m * total + sides * d * total)),
        name="outer",
    )(pick, *args)


TILE = 128


def whole(v):
    return pl.BlockSpec((TILE, v.shape[1]), lambda i: (i, 0))


def vector(v):
    return pl.BlockSpec(v.shape, lambda i: (0, 0))


def halves(v):
    count = v.shape[0] // TILE
    return (
        pl.BlockSpec((TILE, v.shape[1]), lambda i: (jnp.minimum(i, count - 1), 0)),
        pl.BlockSpec((TILE, v.shape[1]), lambda i: (jnp.maximum(i - count, 0), 0)),
    )


def in_half(count, use):
    for side in range(2):
        pl.when(pl.program_id(0) // count == side)(functools.partial(use, side))


def total_of(terms, side):
    picked = [t[...].astype(F32) for t in terms[3 * side : 3 * side + 3]]
    return picked[0] + picked[1] + picked[2]


def unit(values):
    center = values - jnp.mean(values, axis=-1, keepdims=True)
    factor = lax.rsqrt(jnp.mean(center * center, axis=-1, keepdims=True) + 1e-05)
    return center * factor, factor


def unit_back(tangent, gain, xhat, factor):
    e = tangent * gain
    return factor * (
        e - jnp.mean(e, axis=-1, keepdims=True) - xhat * jnp.mean(e * xhat, axis=-1, keepdims=True)
    )


def add_sums(s_ref, rows):
    sums = jnp.concatenate([jnp.sum(r, axis=0, keepdims=True) for r in rows], axis=0)
    first = pl.program_id(0) == 0

    @pl.when(first)
    def _():
        s_ref[0 : len(rows), :] = sums

    @pl.when(jnp.logical_not(first))
    def _():
        s_ref[0 : len(rows), :] += sums


def first_kernel(count, x_ref, gain_ref, shift_ref, *outs):
    def use(side):
        xhat, _ = unit(x_ref[...].astype(F32))
        outs[side][...] = (xhat * gain_ref[...] + shift_ref[...]).astype(BF)

    in_half(count, use)


def middle_kernel(count, *refs):
    terms, (x_ref, bias_ref, gain_ref, shift_ref, m_ref), outs = refs[:6], refs[6:11], refs[11:]

    def use(side):
        middle = x_ref[...].astype(F32) + total_of(terms, side) + bias_ref[...]
        m_ref[...] = middle
        xhat, _ = unit(middle)
        outs[side][...] = (xhat * gain_ref[...] + shift_ref[...]).astype(BF)

    in_half(count, use)


def output_kernel(count, *refs):
    terms, (m_ref, live_ref, bias_ref, o_ref) = refs[:6], refs[6:]

    def use(side):
        o_ref[...] = (live_ref[:, 0:1] * (m_ref[...] + total_of(terms, side) + bias_ref[...])).astype(BF)

    in_half(count, use)


def middle_back_kernel(count, *refs):
    terms, (m_ref, g_ref, live_ref, gain_ref, b_ref, s_ref), outs = refs[:6], refs[6:12], refs[12:]

    def use(side):
        tangent = total_of(terms, side)
        xhat, factor = unit(m_ref[...])
        upstream = live_ref[:, 0:1] * g_ref[...].astype(F32)
        back = upstream + unit_back(tangent, gain_ref[...], xhat, factor)
        b_ref[...] = back
        outs[side][...] = back.astype(BF)
        add_sums(s_ref, [tangent * xhat, tangent, back, upstream])

    in_half(count, use)


def input_back_kernel(count, *refs):
    terms, (x_ref, b_ref, gain_ref, o_ref, s_ref) = refs[:6], refs[6:]

    def use(side):
        tangent = total_of(terms, side)
        xhat, factor = unit(x_ref[...].astype(F32))
        o_ref[...] = (b_ref[...] + unit_back(tangent, gain_ref[...], xhat, factor)).astype(BF)
        add_sums(s_ref, [tangent * xhat, tangent])

    in_half(count, use)


def over_rows(kernel, terms, rows, vectors, wholes=(), pieces=0, sums=False):
    m = rows[0].shape[0]
    d = rows[0].shape[1]
    half = jax.ShapeDtypeStruct((m // 2, d), BF)
    upper, lower = halves(half)
    specs = [upper] * 3 + [lower] * 3 if terms else []
    specs += [whole(r) for r in rows] + [vector(v) for v in vectors]
    outs = [jax.ShapeDtypeStruct((m, d), t) for t in wholes]
    out_specs = [whole(o) for o in outs]
    if sums:
        outs.append(jax.ShapeDtypeStruct((8, d), F32))
        out_specs.append(vector(outs[-1]))
    outs += [half] * pieces
    out_specs += [upper, lower][:pieces]
    return pl.pallas_call(
        functools.partial(kernel, m // 2 // TILE),
        grid=(m // TILE,),
        in_specs=specs,
        out_specs=out_specs,
        out_shape=outs,
        compiler_params=params(),
        cost_estimate=cost(20 * m * d, 16 * m * d),
        name=kernel.__name__.replace("_kernel", ""),
    )(*terms, *rows, *vectors)


def assemble_kernel(own_ref, *refs):
    pieces, o_ref, sems = refs[:8], refs[8], refs[9]
    rows = pieces[0].shape[0]
    for side in range(2):

        @pl.when(own_ref[0] == 1 - side)
        def _():
            copies = [
                pltpu.make_async_copy(pieces[4 * side + k], o_ref.at[pl.ds(k * rows, rows), :], sems.at[k])
                for k in range(4)
            ]
            for c in copies:
                c.start()
            for c in copies:
                c.wait()


def assemble(own, mine, theirs):
    rows, d = mine[0].shape
    anywhere = pl.BlockSpec(memory_space=pl.ANY)
    return pl.pallas_call(
        assemble_kernel,
        in_specs=[pl.BlockSpec(memory_space=pltpu.SMEM)] + [anywhere] * 8,
        out_specs=pl.BlockSpec(memory_space=pltpu.VMEM),
        out_shape=jax.ShapeDtypeStruct((4 * rows, d), BF),
        scratch_shapes=[pltpu.SemaphoreType.DMA((4,))],
        compiler_params=params(16),
        cost_estimate=cost(0, 16 * rows * d),
        name="assemble",
    )(own, *mine, *theirs)


def place_kernel(plane_ref, *refs):
    for k in range(4):

        @pl.when(pl.program_id(0) == k)
        def _():
            start = 0
            for o_ref in refs[4:]:
                if len(o_ref.shape) == 3:
                    width = o_ref.shape[2]
                    for j in range(o_ref.shape[0]):
                        o_ref[j] = refs[k][:, start : start + width].astype(o_ref.dtype)
                        start += width
                else:
                    width = o_ref.shape[1]
                    o_ref[...] = refs[k][:, start : start + width].astype(o_ref.dtype)
                    start += width


def place(plane, pieces, axis, dtype, split=(1,)):
    m, n = pieces[0].shape
    unit_width = n // sum(split)
    outs, specs = [], []
    for count in split:
        if axis == 0:
            outs.append(jax.ShapeDtypeStruct((4 * m, n), dtype))
            specs.append(pl.BlockSpec((m, n), lambda k, p: (p[0] ^ k, 0)))
        elif count == 1:
            outs.append(jax.ShapeDtypeStruct((m, 4 * unit_width), dtype))
            specs.append(pl.BlockSpec((m, unit_width), lambda k, p: (0, p[0] ^ k)))
        else:
            outs.append(jax.ShapeDtypeStruct((count, m, 4 * unit_width), dtype))
            specs.append(pl.BlockSpec((count, m, unit_width), lambda k, p: (0, 0, p[0] ^ k)))
    return pl.pallas_call(
        place_kernel,
        grid_spec=pltpu.PrefetchScalarGridSpec(
            num_scalar_prefetch=1,
            grid=(4,),
            in_specs=[pl.BlockSpec((m, n), lambda k, p: (0, 0))] * 4,
            out_specs=specs,
        ),
        out_shape=outs,
        compiler_params=params(),
        cost_estimate=cost(0, 16 * m * n),
        name="place",
    )(plane, *pieces)


def part_kernel(plane_ref, v_ref, *outs):
    for k in range(4):

        @pl.when(pl.program_id(0) == k)
        def _():
            outs[k][...] = v_ref[...]


def part_rows(plane, v):
    m, n = v.shape[0] // 4, v.shape[1]
    return pl.pallas_call(
        part_kernel,
        grid_spec=pltpu.PrefetchScalarGridSpec(
            num_scalar_prefetch=1,
            grid=(4,),
            in_specs=[pl.BlockSpec((m, n), lambda k, p: (p[0] ^ k, 0))],
            out_specs=[pl.BlockSpec((m, n), lambda k, p: (0, 0))] * 4,
        ),
        out_shape=[jax.ShapeDtypeStruct((m, n), v.dtype)] * 4,
        compiler_params=params(),
        cost_estimate=cost(0, 16 * m * n),
        name="part_rows",
    )(plane, v)


def after(value, *others):
    return lax.optimization_barrier((value, *others))[0]


def body(
    depth,
    inputs,
    gamma_first,
    beta_first,
    heads_weight,
    output_weight,
    output_bias,
    gamma_second,
    beta_second,
    expand_weight,
    expand_bias,
    reduce_weight,
    reduce_bias,
    group_sizes,
    prefix_lengths,
    solution_lengths,
    cotangent,
):
    block, model = inputs.shape
    zi, yi, xi, ci = (lax.axis_index(a) for a in ALL)
    plane = yi * 2 + xi
    own = xi == ci
    send = lambda v, route: lax.ppermute(v, ALL, pairs_of(depth, route))
    wide = lambda v: v.astype(F32)

    def near_of(v):
        return send(v, lambda y, x, c: (y, x, c) if c == x else (y, 1 - x, 1 - c))

    def far_of(v):
        return send(v, lambda y, x, c: (1 - y, x, c) if c == x else (1 - y, 1 - x, 1 - c))

    flip_y = lambda y, x, c: (1 - y, x, c)
    owners_y = lambda y, x, c: (1 - y, x, c) if c == x else None
    others_y = lambda y, x, c: (1 - y, x, c) if c != x else None
    owners_x = lambda y, x, c: (y, 1 - x, c) if c == x else None
    others_x = lambda y, x, c: (y, 1 - x, c) if c != x else None

    def spread_out(top, low):
        y_low, x_top = send(low, owners_y), send(top, owners_x)
        return top, low, send(top, owners_y), y_low, x_top, send(low, owners_x)

    def spread_on(moved):
        top, low, y_top, y_low, x_top, x_low = moved
        far_low, far_top = send(y_low, owners_x), send(x_top, others_y)
        return assemble(own_flag, (top, low, y_top, y_low), (x_top, x_low, far_top, far_low))

    def collect(far, near, *work):
        far_top, far_low = far
        near_top, near_low = near
        by_y, to_far = send(far_top, flip_y), send(far_low, others_x)
        by_x = send(near_low, others_x)
        ahead_y, ahead_x, *_ = lax.optimization_barrier((to_far, by_y, *work))
        from_y = send((wide(far_low) + wide(ahead_y)).astype(BF), owners_y)
        from_x = send((wide(near_top) + wide(ahead_x)).astype(BF), others_x)
        return (near_top, from_x, by_y, near_low, by_x, from_y), (to_far, by_y)

    def from_owner(v):
        return jnp.where(own, v, send(v, lambda y, x, c: (y, x, 1 - c) if c == x else None))

    def shuffle(pieces, *first):
        routes = (
            lambda y, x, c: (y, 1 - x, c),
            lambda y, x, c: (1 - y, x, c),
            lambda y, x, c: (1 - y, 1 - x, c),
        )
        pieces = lax.optimization_barrier((*pieces, *first))[:4]
        return [pieces[0]] + [send(pieces[k], routes[k - 1]) for k in (1, 2, 3)]

    def columns(v, k):
        width = v.shape[-1] // 4
        return lax.dynamic_slice_in_dim(v, (plane ^ k) * width, width, axis=-1)

    def gather(pieces):
        full = lax.all_gather(place(plane_flag, pieces, 0, BF)[0], ("c", "z"), axis=0, tiled=True)
        return full.reshape(2, full.shape[0] // 2, full.shape[1])

    def scatter(terms, axes):
        return lax.psum_scatter(terms.reshape(-1, terms.shape[-1]), axes, scatter_dimension=0, tiled=True)

    pick = ci.astype(jnp.int32).reshape(1)
    plane_flag = plane.astype(jnp.int32).reshape(1)
    own_flag = own.astype(jnp.int32).reshape(1)
    row = lambda v: wide(v).reshape(1, -1)
    shard, _, local = heads_weight.shape
    part = local // 4
    inner = expand_weight.shape[1] // 4

    def attention_columns(k):
        heads = columns(heads_weight, k)
        return jnp.concatenate([heads[:, 0], heads[:, 1], heads[:, 2], columns(output_weight, k)], axis=1)

    heads_got = shuffle([attention_columns(k) for k in range(4)])
    heads_all = gather(heads_got)

    info, live = bounds_of(group_sizes, prefix_lengths, solution_lengths, block)
    info = jnp.pad(info, ((0, 0), (0, 5)))
    live_mask = wide(live)[:, None]
    live_wide = jnp.broadcast_to(live_mask, (block, 128))
    info_two = jnp.concatenate([near_of(info), far_of(info)], axis=0)
    first_own = over_rows(first_kernel, (), (inputs,), (row(gamma_first), row(beta_first)), pieces=2)
    first_own = lax.optimization_barrier((*first_own, *heads_got))[:2]
    first = spread_on(spread_out(*first_own))

    expand_got = shuffle([columns(expand_weight, k) for k in range(4)], first)
    expand_all = gather(expand_got)
    reduce_got = shuffle([columns(reduce_weight, k) for k in range(4)], *expand_got)
    reduce_all = gather(reduce_got)
    bias_mine = lax.dynamic_slice_in_dim(expand_bias, plane * inner, inner).reshape(1, 1, inner)
    bias_other = send(bias_mine, lambda y, x, c: (y, x, 1 - c))
    bias = wide(
        jnp.where(ci == 0, jnp.concatenate([bias_mine, bias_other]), jnp.concatenate([bias_other, bias_mine]))
    )
    upstream_own = (live_mask * wide(cotangent)).astype(BF)
    upstream_own = (upstream_own[: block // 2], upstream_own[block // 2 :])

    both = jnp.arange(2, dtype=jnp.int32)
    projected = project(first, heads_all, 3 * part, 0)
    mixed, log_sums = attend(info_two, projected, block)
    far = contract(mixed, heads_all, 3, 1)
    attended, _ = collect(far, contract(after(mixed, *far), heads_all, 3, 0))
    middle, *second_own = over_rows(
        middle_kernel, attended, (inputs,), (row(output_bias), row(gamma_second), row(beta_second)), (F32,), pieces=2
    )
    second = spread_on(spread_out(*second_own))
    upstream_low = spread_on(spread_out(*lax.optimization_barrier((*upstream_own, second))[:2]))
    activated, slope = expand(second, expand_all, bias)
    reduce_terms = outer(both, [(upstream_low, activated)], depth)
    reduce_part = scatter(reduce_terms, ("z", "c"))

    slope, upstream_last, _ = lax.optimization_barrier((slope, upstream_low, reduce_terms))
    sum_low, expand_bias_gradient = expand_back(upstream_last, reduce_all, slope)
    expand_bias_gradient = expand_bias_gradient.reshape(2, inner)
    far, near = contract(sum_low, expand_all, 0, 1), contract(sum_low, expand_all, 0, 0)
    expand_terms = outer(both, [(second, after(sum_low, *far, *near))], depth)
    second_back, _ = collect(far, near, expand_terms)
    expand_part = scatter(expand_terms, ("z", "c"))
    second_back = lax.optimization_barrier((*second_back, expand_terms))[:6]
    middle_back, sums_second, *middle_own = over_rows(
        middle_back_kernel,
        second_back,
        (middle, cotangent, live_wide),
        (row(gamma_second),),
        (F32,),
        pieces=2,
        sums=True,
    )
    active_last = after(activated, *middle_own)
    far, near = contract(active_last, reduce_all, 0, 1), contract(active_last, reduce_all, 0, 0)
    middle_low = spread_on(spread_out(*middle_own))
    terms = lax.optimization_barrier((*far, *near, middle_low))
    branch, moved = collect(terms[:2], terms[2:4])

    mixed_back = project(after(middle_low, reduce_part, *far, *near), heads_all, part, 3)
    projected_back = attend_back(info_two, projected, mixed_back, log_sums, block)
    far = contract(projected_back, heads_all, 0, 1)
    near = contract(after(projected_back, *far, *moved), heads_all, 0, 0)
    first_back, ahead = collect(far, near)
    heads_terms = outer(both, [(first, after(projected_back, *near, *ahead)), (middle_low, mixed)], depth)
    heads_part = scatter(after(heads_terms, expand_part), ("z", "c"))
    reduce_got = shuffle(part_rows(plane_flag, reduce_part), *far, *near)
    (outputs,) = over_rows(output_kernel, branch, (middle, live_wide), (row(reduce_bias),), (BF,))
    outputs = from_owner(outputs)
    (reduce_gradient,) = place(plane_flag, reduce_got, 1, F32)
    input_gradient, sums_first = over_rows(
        input_back_kernel, first_back, (inputs, middle_back), (row(gamma_first),), (BF,), sums=True
    )
    input_gradient = from_owner(input_gradient)

    expand_got = shuffle(part_rows(plane_flag, expand_part), *first_back)
    (expand_gradient,) = place(plane_flag, expand_got, 1, F32)
    gamma_first_gradient, beta_first_gradient = sums_first[0], sums_first[1]
    gamma_second_gradient, beta_second_gradient = sums_second[0], sums_second[1]
    output_bias_gradient, reduce_bias_gradient = sums_second[2], sums_second[3]

    vectors = jnp.stack(
        [
            gamma_first_gradient,
            beta_first_gradient,
            output_bias_gradient,
            gamma_second_gradient,
            beta_second_gradient,
            reduce_bias_gradient,
        ]
    )
    vectors = jnp.where(own, vectors, 0.0)
    placed = lax.dynamic_update_slice(jnp.zeros((2, 4 * inner), F32), expand_bias_gradient, (0, plane * inner))
    sums = jnp.concatenate([vectors.reshape(-1), placed.reshape(-1)]).reshape(-1, 128)
    for route in (
        lambda y, x, c: (y, x, 1 - c),
        lambda y, x, c: (y, 1 - x, c),
        lambda y, x, c: (1 - y, x, c),
    ):
        sums = sums + send(sums, route)
    step = 1
    while step < depth:
        sums = sums + lax.ppermute(sums, "z", [(i, i ^ step) for i in range(depth)])
        step *= 2
    flat = sums.reshape(-1)
    index = zi * 4 + plane
    vectors = lax.dynamic_slice_in_dim(flat[: 6 * model].reshape(6, model), index * shard, shard, axis=1)
    placed = flat[6 * model :].reshape(2, 4 * inner)
    count = 4 * inner // (4 * depth)
    expand_bias_gradient = lax.dynamic_slice(placed, (ci, index * count), (1, count))
    heads_part, reduce_gradient, expand_gradient, outputs, input_gradient, vectors, expand_bias_gradient = (
        lax.optimization_barrier(
            (heads_part, reduce_gradient, expand_gradient, outputs, input_gradient, vectors, expand_bias_gradient)
        )
    )
    heads_got = shuffle(part_rows(plane_flag, heads_part))
    heads_gradient, output_gradient = place(plane_flag, heads_got, 1, F32, (3, 1))
    heads_gradient = heads_gradient.transpose(1, 0, 2)
    return (
        outputs,
        input_gradient,
        vectors[0],
        vectors[1],
        heads_gradient,
        output_gradient,
        vectors[2],
        vectors[3],
        vectors[4],
        expand_gradient,
        expand_bias_gradient,
        reduce_gradient,
        vectors[5],
    )


def solution(mesh):
    depth = mesh.shape["dp"] // 4
    fine = Mesh(mesh.devices.reshape(depth, 2, 2, 2), ALL)
    dp = ("z", "y", "x")
    placed = (
        P(dp, None),
        P(),
        P(),
        P(dp, None, "c"),
        P(dp, "c"),
        P(),
        P(),
        P(),
        P(dp, "c"),
        P("c"),
        P(dp, "c"),
        P(),
        P(dp),
        P(dp),
        P(dp, None),
        P(dp, None),
    )
    return jax.shard_map(
        functools.partial(body, depth),
        mesh=fine,
        in_specs=placed,
        out_specs=(
            P(dp, None),
            P(dp, None),
            P(dp),
            P(dp),
            P(dp, None, "c"),
            P(dp, "c"),
            P(dp),
            P(dp),
            P(dp),
            P(dp, "c"),
            P("c", dp),
            P(dp, "c"),
            P(dp),
        ),
        check_vma=False,
    )
```

```python
import functools

import jax
import jax.numpy as jnp
from jax import lax
from jax.experimental import pallas as pl
from jax.experimental.pallas import tpu as pltpu
from jax.sharding import Mesh
from jax.sharding import PartitionSpec as P

HEAD = 128
WINDOW = 256
CHUNK = 128
SCALE = HEAD**-0.5
ALL = ("z", "y", "x", "c")
BF = jnp.bfloat16
F32 = jnp.float32
ACROSS = (((1,), (1,)), ((), ()))
ROWS = (((0,), (0,)), ((), ()))
PLAIN = (((1,), (0,)), ((), ()))


def dot(a, b, dims=PLAIN):
    return lax.dot_general(a, b, dims, preferred_element_type=F32)


def pairs_of(depth, route):
    def flat(z, y, x, c):
        return ((z * 2 + y) * 2 + x) * 2 + c

    found = []
    for z in range(depth):
        for y in range(2):
            for x in range(2):
                for c in range(2):
                    goal = route(y, x, c)
                    if goal is not None:
                        found.append((flat(z, y, x, c), flat(z, *goal)))
    return found


def bounds_of(group_sizes, prefix_lengths, solution_lengths, row_count):
    entries = solution_lengths.shape[1]
    position = jnp.arange(entries, dtype=jnp.int32)
    counted = jnp.where(position[None, :] < group_sizes[:, None], solution_lengths, 0)
    pieces = jnp.concatenate([prefix_lengths[:, None], counted], axis=1)
    flat = pieces.reshape(-1)
    count = flat.shape[0]
    index = jnp.arange(count, dtype=jnp.int32)
    ends = jnp.sum(jnp.where(index[None, :] <= index[:, None], flat[None, :], 0), axis=1)
    slot = jnp.arange(row_count, dtype=jnp.int32)
    passed = slot[:, None] >= ends[None, :]
    piece_start = jnp.max(jnp.where(passed, ends[None, :], 0), axis=1)
    group_end = ends.reshape(pieces.shape)[:, -1]
    over = slot[:, None] >= group_end[None, :]
    group_start = jnp.max(jnp.where(over, group_end[None, :], 0), axis=1)
    group_index = jnp.sum(over.astype(jnp.int32), axis=1)
    member = group_index[:, None] == jnp.arange(pieces.shape[0], dtype=jnp.int32)[None, :]
    prefix_end = group_start + jnp.sum(jnp.where(member, prefix_lengths[None, :], 0), axis=1)
    live = slot < ends[-1]
    piece_start = jnp.where(live, piece_start, slot)
    group_start = jnp.where(live, group_start, slot)
    prefix_end = jnp.where(live, prefix_end, slot)
    return jnp.stack([group_start, prefix_end, piece_start], axis=1), live


def key_range(i):
    return max(0, i * CHUNK - WINDOW), (i + 1) * CHUNK


def allowed_tile(info, i, lo, hi):
    rows = info[i * CHUNK : (i + 1) * CHUNK, :]
    start, stop, piece = rows[:, 0:1], rows[:, 1:2], rows[:, 2:3]
    s = lax.broadcasted_iota(jnp.int32, (CHUNK, hi - lo), 0) + i * CHUNK
    t = lax.broadcasted_iota(jnp.int32, (CHUNK, hi - lo), 1) + lo
    return (t <= s) & ((t >= piece) | ((t >= start) & (t < stop)))


def tiles_of(p_ref, width):
    found = []
    for i in range(p_ref.shape[0] // CHUNK):
        lo, hi = key_range(i)
        rows = slice(i * CHUNK, (i + 1) * CHUNK)
        for h in range(width // HEAD):
            qs, ks, vs = (slice(c * width + h * HEAD, c * width + (h + 1) * HEAD) for c in range(3))
            found.append((i, rows, slice(lo, hi), qs, ks, vs))
    return found


def masks_of(info_ref, block):
    info = info_ref[...]
    return [allowed_tile(info, i, *key_range(i)) for i in range(block // CHUNK)]


def attend_kernel(info_ref, p_ref, o_ref, l_ref):
    block, width = p_ref.shape
    width = width // 3
    masks = masks_of(info_ref, block)
    tiles = tiles_of(p_ref, width)
    raw = [dot(p_ref[rows, qs], p_ref[keys, ks], ACROSS) for _, rows, keys, qs, ks, _ in tiles]
    low = []
    for (i, rows, _, qs, _, _), score in zip(tiles, raw):
        scores = jnp.where(masks[i], score * SCALE, -1e30)
        peak = jnp.max(scores, axis=-1, keepdims=True)
        e = jnp.exp(scores - peak)
        total = jnp.sum(e, axis=-1, keepdims=True)
        low.append((e * (1.0 / total)).astype(BF))
        l_ref[rows, qs] = jnp.broadcast_to(peak + jnp.log(total), (CHUNK, HEAD))
    for (_, rows, keys, qs, _, vs), soft in zip(tiles, low):
        o_ref[rows, qs] = dot(soft, p_ref[keys, vs]).astype(BF)


def attend_back_kernel(info_ref, p_ref, g_ref, l_ref, d_ref, dk_ref, dv_ref):
    block, width = p_ref.shape
    width = width // 3
    masks = masks_of(info_ref, block)
    tiles = tiles_of(p_ref, width)
    dk_ref[...] = jnp.zeros_like(dk_ref)
    dv_ref[...] = jnp.zeros_like(dv_ref)
    raw = [dot(p_ref[rows, qs], p_ref[keys, ks], ACROSS) for _, rows, keys, qs, ks, _ in tiles]
    tangents = [dot(g_ref[rows, qs], p_ref[keys, vs], ACROSS) for _, rows, keys, qs, _, vs in tiles]
    kept = []
    for (i, rows, _, qs, _, _), score, tangent in zip(tiles, raw, tangents):
        scores = jnp.where(masks[i], score * SCALE, -1e30)
        soft = jnp.exp(scores - l_ref[rows, qs.start : qs.start + 1])
        back = soft * tangent
        low = (back - soft * jnp.sum(back, axis=-1, keepdims=True)).astype(BF)
        kept.append((soft.astype(BF), low))
    for (_, rows, keys, qs, ks, _), (soft, low) in zip(tiles, kept):
        d_ref[rows, qs] = (dot(low, p_ref[keys, ks]) * SCALE).astype(BF)
        dk_ref[keys, qs] += dot(low, p_ref[rows, qs], ROWS)
        dv_ref[keys, qs] += dot(soft, g_ref[rows, qs], ROWS)
    d_ref[:, width : 2 * width] = (dk_ref[...] * SCALE).astype(BF)
    d_ref[:, 2 * width :] = dv_ref[...].astype(BF)


def params(mib=48):
    return pltpu.CompilerParams(vmem_limit_bytes=mib << 20)


def cost(flops, moved, exps=0):
    return pl.CostEstimate(flops=flops * 4, bytes_accessed=moved * 4, transcendentals=exps)


def attend(info, projected, block):
    sides, rows, width = projected.shape
    spec = lambda n: pl.BlockSpec((None, block, n), lambda b, c: (c, b, 0))
    return pl.pallas_call(
        attend_kernel,
        grid=(rows // block, sides),
        in_specs=[pl.BlockSpec((block, info.shape[1]), lambda b, c: (b, 0)), spec(width)],
        out_specs=[spec(width // 3)] * 2,
        out_shape=[jax.ShapeDtypeStruct((sides, rows, width // 3), t) for t in (BF, F32)],
        compiler_params=params(16),
        cost_estimate=cost(16 * rows * block * width, 8 * rows * width * 2, rows * block * 4),
        name="attend",
    )(info, projected)


def attend_back(info, projected, mixed_back, log_sums, block):
    sides, rows, width = projected.shape
    spec = lambda n: pl.BlockSpec((None, block, n), lambda b, c: (c, b, 0))
    return pl.pallas_call(
        attend_back_kernel,
        grid=(rows // block, sides),
        in_specs=[pl.BlockSpec((block, info.shape[1]), lambda b, c: (b, 0)), spec(width), spec(width // 3), spec(width // 3)],
        out_specs=spec(width),
        out_shape=jax.ShapeDtypeStruct((sides, rows, width), BF),
        scratch_shapes=[pltpu.VMEM((block, width // 3), F32)] * 2,
        compiler_params=params(20),
        cost_estimate=cost(40 * rows * block * width, 16 * rows * width * 2, rows * block * 4),
        name="attend_back",
    )(info, projected, mixed_back, log_sums)


def steps(width, step=256):
    return [slice(j, min(j + step, width)) for j in range(0, width, step)]


def far_away(v):
    return pltpu.with_memory_space_constraint(v, pltpu.HBM)


def project_kernel(a_ref, w_ref, o_ref):
    for s in steps(w_ref.shape[1]):
        o_ref[:, s] = dot(a_ref[...], w_ref[:, s]).astype(BF)


def project(rows, weights, width, column):
    m, k = rows.shape
    sides = weights.shape[0]
    return pl.pallas_call(
        project_kernel,
        grid=(sides,),
        in_specs=[pl.BlockSpec((m, k), lambda c: (0, 0)), pl.BlockSpec((None, k, width), lambda c: (c, 0, column))],
        out_specs=pl.BlockSpec((None, m, width), lambda c: (c, 0, 0)),
        out_shape=jax.ShapeDtypeStruct((sides, m, width), BF),
        compiler_params=params(24),
        cost_estimate=cost(2 * sides * m * k * width, 2 * (m * k + sides * k * width + sides * m * width)),
        name="project",
    )(far_away(rows), far_away(weights))


def expand_kernel(a_ref, w_ref, b_ref, o_ref, d_ref):
    root, cubic = 0.7978845608028654, 0.044715
    for s in steps(w_ref.shape[1]):
        v = dot(a_ref[...], w_ref[:, s]) + b_ref[:, s]
        square = v * v
        t = jnp.tanh(v * (root + root * cubic * square))
        half = 0.5 + 0.5 * t
        o_ref[:, s] = (v * half).astype(BF)
        d_ref[:, s] = half + v * (half * (1.0 - t)) * (root + 3.0 * root * cubic * square)


def expand(rows, weights, bias):
    m, k = rows.shape
    sides, _, n = weights.shape
    tile = min(n, 256)
    out = pl.BlockSpec((None, m, tile), lambda c, j: (c, 0, j))
    return pl.pallas_call(
        expand_kernel,
        grid=(sides, n // tile),
        in_specs=[
            pl.BlockSpec((m, k), lambda c, j: (0, 0)),
            pl.BlockSpec((None, k, tile), lambda c, j: (c, 0, j)),
            pl.BlockSpec((None, 1, tile), lambda c, j: (c, 0, j)),
        ],
        out_specs=[out, out],
        out_shape=[jax.ShapeDtypeStruct((sides, m, n), BF), jax.ShapeDtypeStruct((sides, m, n), F32)],
        compiler_params=params(24),
        cost_estimate=cost(2 * sides * m * k * n, 2 * (m * k + sides * k * n) + 6 * sides * m * n, sides * m * n),
        name="expand",
    )(far_away(rows), far_away(weights), bias)


def expand_back_kernel(a_ref, w_ref, d_ref, o_ref, s_ref):
    for s in steps(w_ref.shape[1]):
        back = dot(a_ref[...], w_ref[:, s]) * d_ref[:, s]
        o_ref[:, s] = back.astype(BF)
        s_ref[:, s] = jnp.sum(back, axis=0, keepdims=True)


def expand_back(rows, weights, slope):
    m, k = rows.shape
    sides, _, n = weights.shape
    tile = min(n, 512)
    out = pl.BlockSpec((None, m, tile), lambda c, j: (c, 0, j))
    return pl.pallas_call(
        expand_back_kernel,
        grid=(sides, n // tile),
        in_specs=[
            pl.BlockSpec((m, k), lambda c, j: (0, 0)),
            pl.BlockSpec((None, k, tile), lambda c, j: (c, 0, j)),
            out,
        ],
        out_specs=[out, pl.BlockSpec((None, 1, tile), lambda c, j: (c, 0, j))],
        out_shape=[jax.ShapeDtypeStruct((sides, m, n), BF), jax.ShapeDtypeStruct((sides, 1, n), F32)],
        compiler_params=params(24),
        cost_estimate=cost(2 * sides * m * k * n, 2 * (m * k + sides * k * n) + 6 * sides * m * n),
        name="expand_back",
    )(far_away(rows), far_away(weights), far_away(slope))


def contract_kernel(a_ref, w_ref, top_ref, low_ref):
    half = top_ref.shape[0]
    for s in steps(w_ref.shape[1]):
        total = dot(a_ref[0], w_ref[0, s, :], ACROSS)
        for c in range(1, a_ref.shape[0]):
            total = total + dot(a_ref[c], w_ref[c, s, :], ACROSS)
        top_ref[:, s] = total[:half].astype(BF)
        low_ref[:, s] = total[half:].astype(BF)


def contract(terms, weights, column, side):
    sides, m, n = terms.shape
    d = weights.shape[1]
    m = m // 2
    tile = min(d, 512)
    half = pl.BlockSpec((m // 2, tile), lambda j: (0, j))
    out = jax.ShapeDtypeStruct((m // 2, d), BF)
    return pl.pallas_call(
        contract_kernel,
        grid=(d // tile,),
        in_specs=[
            pl.BlockSpec((sides, m, n), lambda j: (0, side, 0)),
            pl.BlockSpec((sides, tile, n), lambda j: (0, j, column)),
        ],
        out_specs=[half, half],
        out_shape=[out, out],
        compiler_params=params(16),
        cost_estimate=cost(2 * sides * m * n * d, 2 * (sides * m * n + sides * n * d + m * d)),
        name="contract",
    )(terms, far_away(weights))


def outer_kernel(pairs, adds, pick_ref, *refs):
    o_ref = refs[-1]
    start = 0
    for i in range(pairs):
        a_ref, r_ref = refs[2 * i], refs[2 * i + 1]
        for s in steps(r_ref.shape[1]):
            place = slice(start + s.start, start + s.stop)
            total = dot(a_ref[...], r_ref[:, s], ROWS)
            if adds:
                total = total + refs[2 * pairs][:, place].astype(F32)
            o_ref[:, place] = total.astype(BF)
        start += r_ref.shape[1]


def outer(pick, pairs, depth, extra=None):
    m, d = pairs[0][0].shape
    sides = pick.shape[0]
    total = sum(r.shape[2] for _, r in pairs)
    tile = d // depth
    place = pl.BlockSpec((None, None, tile, total), lambda c, i, s: (i, c, 0, 0))
    specs, args = [], []
    for a, r in pairs:
        specs.append(pl.BlockSpec((m, tile), lambda c, i, s: (0, i)))
        specs.append(pl.BlockSpec((None, m, r.shape[2]), lambda c, i, s: (s[c], 0, 0)))
        args += [a, r]
    if extra is not None:
        specs.append(place)
        args.append(extra)
    return pl.pallas_call(
        functools.partial(outer_kernel, len(pairs), extra is not None),
        grid_spec=pltpu.PrefetchScalarGridSpec(
            num_scalar_prefetch=1, grid=(sides, depth), in_specs=specs, out_specs=place
        ),
        out_shape=pltpu.HBM((depth, sides, tile, total), BF),
        compiler_params=params(16),
        cost_estimate=cost(4 * sides * m * d * total, 4 * (m * d + sides * m * total + sides * d * total)),
        name="outer",
    )(pick, *args)


TILE = 128


def whole(v):
    return pl.BlockSpec((TILE, v.shape[1]), lambda i: (i, 0))


def vector(v):
    return pl.BlockSpec(v.shape, lambda i: (0, 0))


def halves(v):
    count = v.shape[0] // TILE
    return (
        pl.BlockSpec((TILE, v.shape[1]), lambda i: (jnp.minimum(i, count - 1), 0)),
        pl.BlockSpec((TILE, v.shape[1]), lambda i: (jnp.maximum(i - count, 0), 0)),
    )


def in_half(count, use):
    for side in range(2):
        pl.when(pl.program_id(0) // count == side)(functools.partial(use, side))


def total_of(terms, side):
    picked = [t[...].astype(F32) for t in terms[3 * side : 3 * side + 3]]
    return picked[0] + picked[1] + picked[2]


def unit(values):
    center = values - jnp.mean(values, axis=-1, keepdims=True)
    factor = lax.rsqrt(jnp.mean(center * center, axis=-1, keepdims=True) + 1e-05)
    return center * factor, factor


def unit_back(tangent, gain, xhat, factor):
    e = tangent * gain
    return factor * (
        e - jnp.mean(e, axis=-1, keepdims=True) - xhat * jnp.mean(e * xhat, axis=-1, keepdims=True)
    )


def add_sums(s_ref, rows):
    sums = jnp.concatenate([jnp.sum(r, axis=0, keepdims=True) for r in rows], axis=0)
    first = pl.program_id(0) == 0

    @pl.when(first)
    def _():
        s_ref[0 : len(rows), :] = sums

    @pl.when(jnp.logical_not(first))
    def _():
        s_ref[0 : len(rows), :] += sums


def first_kernel(count, x_ref, gain_ref, shift_ref, *outs):
    def use(side):
        xhat, _ = unit(x_ref[...].astype(F32))
        outs[side][...] = (xhat * gain_ref[...] + shift_ref[...]).astype(BF)

    in_half(count, use)


def middle_kernel(count, *refs):
    terms, (x_ref, bias_ref, gain_ref, shift_ref, m_ref), outs = refs[:6], refs[6:11], refs[11:]

    def use(side):
        middle = x_ref[...].astype(F32) + total_of(terms, side) + bias_ref[...]
        m_ref[...] = middle
        xhat, _ = unit(middle)
        outs[side][...] = (xhat * gain_ref[...] + shift_ref[...]).astype(BF)

    in_half(count, use)


def output_kernel(count, *refs):
    terms, (m_ref, live_ref, bias_ref, o_ref) = refs[:6], refs[6:]

    def use(side):
        o_ref[...] = (live_ref[:, 0:1] * (m_ref[...] + total_of(terms, side) + bias_ref[...])).astype(BF)

    in_half(count, use)


def middle_back_kernel(count, *refs):
    terms, (m_ref, g_ref, live_ref, gain_ref, b_ref, s_ref), outs = refs[:6], refs[6:12], refs[12:]

    def use(side):
        tangent = total_of(terms, side)
        xhat, factor = unit(m_ref[...])
        upstream = live_ref[:, 0:1] * g_ref[...].astype(F32)
        back = upstream + unit_back(tangent, gain_ref[...], xhat, factor)
        b_ref[...] = back
        outs[side][...] = back.astype(BF)
        add_sums(s_ref, [tangent * xhat, tangent, back, upstream])

    in_half(count, use)


def input_back_kernel(count, *refs):
    terms, (x_ref, b_ref, gain_ref, o_ref, s_ref) = refs[:6], refs[6:]

    def use(side):
        tangent = total_of(terms, side)
        xhat, factor = unit(x_ref[...].astype(F32))
        o_ref[...] = (b_ref[...] + unit_back(tangent, gain_ref[...], xhat, factor)).astype(BF)
        add_sums(s_ref, [tangent * xhat, tangent])

    in_half(count, use)


def over_rows(kernel, terms, rows, vectors, wholes=(), pieces=0, sums=False):
    m = rows[0].shape[0]
    d = rows[0].shape[1]
    half = jax.ShapeDtypeStruct((m // 2, d), BF)
    upper, lower = halves(half)
    specs = [upper] * 3 + [lower] * 3 if terms else []
    specs += [whole(r) for r in rows] + [vector(v) for v in vectors]
    outs = [jax.ShapeDtypeStruct((m, d), t) for t in wholes]
    out_specs = [whole(o) for o in outs]
    if sums:
        outs.append(jax.ShapeDtypeStruct((8, d), F32))
        out_specs.append(vector(outs[-1]))
    outs += [half] * pieces
    out_specs += [upper, lower][:pieces]
    return pl.pallas_call(
        functools.partial(kernel, m // 2 // TILE),
        grid=(m // TILE,),
        in_specs=specs,
        out_specs=out_specs,
        out_shape=outs,
        compiler_params=params(24),
        cost_estimate=cost(20 * m * d, 16 * m * d),
        name=kernel.__name__.replace("_kernel", ""),
    )(*terms, *rows, *vectors)


def assemble_kernel(own_ref, *refs):
    pieces, o_ref, sems = refs[:8], refs[8], refs[9]
    rows = pieces[0].shape[0]
    for side in range(2):

        @pl.when(own_ref[0] == 1 - side)
        def _():
            copies = [
                pltpu.make_async_copy(pieces[4 * side + k], o_ref.at[pl.ds(k * rows, rows), :], sems.at[k])
                for k in range(4)
            ]
            for c in copies:
                c.start()
            for c in copies:
                c.wait()


def assemble(own, mine, theirs):
    rows, d = mine[0].shape
    anywhere = pl.BlockSpec(memory_space=pl.ANY)
    return pl.pallas_call(
        assemble_kernel,
        in_specs=[pl.BlockSpec(memory_space=pltpu.SMEM)] + [anywhere] * 8,
        out_specs=pl.BlockSpec(memory_space=pltpu.VMEM),
        out_shape=jax.ShapeDtypeStruct((4 * rows, d), BF),
        scratch_shapes=[pltpu.SemaphoreType.DMA((4,))],
        compiler_params=params(10),
        cost_estimate=cost(0, 16 * rows * d),
        name="assemble",
    )(own, *mine, *theirs)


def place_kernel(plane_ref, *refs):
    for k in range(4):

        @pl.when(pl.program_id(0) == k)
        def _():
            start = 0
            for o_ref in refs[4:]:
                if len(o_ref.shape) == 3:
                    width = o_ref.shape[2]
                    for j in range(o_ref.shape[0]):
                        o_ref[j] = refs[k][:, start : start + width].astype(o_ref.dtype)
                        start += width
                else:
                    width = o_ref.shape[1]
                    o_ref[...] = refs[k][:, start : start + width].astype(o_ref.dtype)
                    start += width


def place(plane, pieces, axis, dtype, split=(1,)):
    m, n = pieces[0].shape
    unit_width = n // sum(split)
    outs, specs = [], []
    for count in split:
        if axis == 0:
            outs.append(jax.ShapeDtypeStruct((4 * m, n), dtype))
            specs.append(pl.BlockSpec((m, n), lambda k, p: (p[0] ^ k, 0)))
        elif count == 1:
            outs.append(jax.ShapeDtypeStruct((m, 4 * unit_width), dtype))
            specs.append(pl.BlockSpec((m, unit_width), lambda k, p: (0, p[0] ^ k)))
        else:
            outs.append(jax.ShapeDtypeStruct((count, m, 4 * unit_width), dtype))
            specs.append(pl.BlockSpec((count, m, unit_width), lambda k, p: (0, 0, p[0] ^ k)))
    return pl.pallas_call(
        place_kernel,
        grid_spec=pltpu.PrefetchScalarGridSpec(
            num_scalar_prefetch=1,
            grid=(4,),
            in_specs=[pl.BlockSpec((m, n), lambda k, p: (0, 0))] * 4,
            out_specs=specs,
        ),
        out_shape=outs,
        compiler_params=params(12),
        cost_estimate=cost(0, 16 * m * n),
        name="place",
    )(plane, *pieces)


def part_kernel(plane_ref, *refs):
    inputs, outs = refs[:-4], refs[-4:]
    for k in range(4):

        @pl.when(pl.program_id(0) == k)
        def _():
            start = 0
            for v_ref in inputs:
                outs[k][:, start : start + v_ref.shape[1]] = v_ref[...]
                start += v_ref.shape[1]


def part_rows(plane, *arrays):
    m, n = arrays[0].shape[0] // 4, sum(v.shape[1] for v in arrays)
    return pl.pallas_call(
        part_kernel,
        grid_spec=pltpu.PrefetchScalarGridSpec(
            num_scalar_prefetch=1,
            grid=(4,),
            in_specs=[pl.BlockSpec((m, v.shape[1]), lambda k, p: (p[0] ^ k, 0)) for v in arrays],
            out_specs=[pl.BlockSpec((m, n), lambda k, p: (0, 0))] * 4,
        ),
        out_shape=[jax.ShapeDtypeStruct((m, n), BF)] * 4,
        compiler_params=params(12),
        cost_estimate=cost(0, 16 * m * n),
        name="part_rows",
    )(plane, *arrays)


def after(value, *others):
    return lax.optimization_barrier((value, *others))[0]


def body(
    depth,
    inputs,
    gamma_first,
    beta_first,
    heads_weight,
    output_weight,
    output_bias,
    gamma_second,
    beta_second,
    expand_weight,
    expand_bias,
    reduce_weight,
    reduce_bias,
    group_sizes,
    prefix_lengths,
    solution_lengths,
    cotangent,
):
    block, model = inputs.shape
    zi, yi, xi, ci = (lax.axis_index(a) for a in ALL)
    plane = yi * 2 + xi
    own = xi == ci
    send = lambda v, route: lax.ppermute(v, ALL, pairs_of(depth, route))
    wide = lambda v: v.astype(F32)

    def near_of(v):
        return send(v, lambda y, x, c: (y, x, c) if c == x else (y, 1 - x, 1 - c))

    def far_of(v):
        return send(v, lambda y, x, c: (1 - y, x, c) if c == x else (1 - y, 1 - x, 1 - c))

    flip_y = lambda y, x, c: (1 - y, x, c)
    owners_y = lambda y, x, c: (1 - y, x, c) if c == x else None
    others_y = lambda y, x, c: (1 - y, x, c) if c != x else None
    owners_x = lambda y, x, c: (y, 1 - x, c) if c == x else None
    others_x = lambda y, x, c: (y, 1 - x, c) if c != x else None

    def spread_out(top, low):
        y_low, x_top = send(low, owners_y), send(top, owners_x)
        return top, low, send(top, owners_y), y_low, x_top, send(low, owners_x)

    def spread_on(moved):
        top, low, y_top, y_low, x_top, x_low = moved
        far_low, far_top = send(y_low, owners_x), send(x_top, others_y)
        return assemble(own_flag, (top, low, y_top, y_low), (x_top, x_low, far_top, far_low))

    def collect(far, near, *work):
        far_top, far_low = far
        near_top, near_low = near
        by_y, to_far = send(far_top, flip_y), send(far_low, others_x)
        by_x = send(near_low, others_x)
        ahead_y, ahead_x, *_ = lax.optimization_barrier((to_far, by_y, *work))
        from_y = send((wide(far_low) + wide(ahead_y)).astype(BF), owners_y)
        from_x = send((wide(near_top) + wide(ahead_x)).astype(BF), others_x)
        return (near_top, from_x, by_y, near_low, by_x, from_y), (to_far, by_y)

    def from_owner(v):
        return jnp.where(own, v, send(v, lambda y, x, c: (y, x, 1 - c) if c == x else None))

    def shuffle(pieces, *first):
        routes = (
            lambda y, x, c: (y, 1 - x, c),
            lambda y, x, c: (1 - y, x, c),
            lambda y, x, c: (1 - y, 1 - x, c),
        )
        pieces = lax.optimization_barrier((*pieces, *first))[:4]
        return [pieces[0]] + [send(pieces[k], routes[k - 1]) for k in (1, 2, 3)]

    def columns(v, k):
        width = v.shape[-1] // 4
        return lax.dynamic_slice_in_dim(v, (plane ^ k) * width, width, axis=-1)

    def placed_rows(pieces):
        return place(plane_flag, pieces, 0, BF)[0]

    def gather(rows):
        full = lax.all_gather(rows, ("c", "z"), axis=0, tiled=True)
        return full.reshape(2, full.shape[0] // 2, full.shape[1])

    def scatter(terms, axes):
        return lax.psum_scatter(terms.reshape(-1, terms.shape[-1]), axes, scatter_dimension=0, tiled=True)

    pick = ci.astype(jnp.int32).reshape(1)
    plane_flag = plane.astype(jnp.int32).reshape(1)
    own_flag = own.astype(jnp.int32).reshape(1)
    row = lambda v: wide(v).reshape(1, -1)
    shard, _, local = heads_weight.shape
    part = local // 4
    inner = expand_weight.shape[1] // 4

    def attention_columns(k):
        heads = columns(heads_weight, k)
        return jnp.concatenate([heads[:, 0], heads[:, 1], heads[:, 2], columns(output_weight, k)], axis=1)

    heads_got = shuffle([attention_columns(k) for k in range(4)])
    heads_all = gather(placed_rows(heads_got))

    info, live = bounds_of(group_sizes, prefix_lengths, solution_lengths, block)
    info = jnp.pad(info, ((0, 0), (0, 5)))
    live_mask = wide(live)[:, None]
    live_wide = jnp.broadcast_to(live_mask, (block, 128))
    info_two = jnp.concatenate([near_of(info), far_of(info)], axis=0)
    first_own = over_rows(first_kernel, (), (inputs,), (row(gamma_first), row(beta_first)), pieces=2)
    first_own = lax.optimization_barrier((*first_own, *heads_got))[:2]
    first = spread_on(spread_out(*first_own))

    expand_got = shuffle([columns(expand_weight, k) for k in range(4)], first)
    expand_all = gather(placed_rows(expand_got))
    reduce_got = shuffle([columns(reduce_weight, k) for k in range(4)], *expand_got)
    reduce_rows = placed_rows(reduce_got)
    bias_mine = lax.dynamic_slice_in_dim(expand_bias, plane * inner, inner).reshape(1, 1, inner)
    bias_other = send(bias_mine, lambda y, x, c: (y, x, 1 - c))
    bias = wide(
        jnp.where(ci == 0, jnp.concatenate([bias_mine, bias_other]), jnp.concatenate([bias_other, bias_mine]))
    )
    upstream_own = (live_mask * wide(cotangent)).astype(BF)
    upstream_own = (upstream_own[: block // 2], upstream_own[block // 2 :])

    both = jnp.arange(2, dtype=jnp.int32)
    first, reduce_rows, bias = lax.optimization_barrier((first, reduce_rows, bias))
    reduce_all = gather(reduce_rows)
    projected = project(first, heads_all, 3 * part, 0)
    mixed, log_sums = attend(info_two, projected, block)
    far = contract(mixed, heads_all, 3, 1)
    attended, _ = collect(far, contract(after(mixed, *far), heads_all, 3, 0))
    middle, *second_own = over_rows(
        middle_kernel, attended, (inputs,), (row(output_bias), row(gamma_second), row(beta_second)), (F32,), pieces=2
    )
    second = spread_on(spread_out(*second_own))
    upstream_low = spread_on(spread_out(*lax.optimization_barrier((*upstream_own, second))[:2]))
    activated, slope = expand(second, expand_all, bias)
    reduce_terms = outer(both, [(upstream_low, activated)], depth)
    reduce_part = scatter(reduce_terms, ("z", "c"))

    slope, upstream_last, _ = lax.optimization_barrier((slope, upstream_low, reduce_terms))
    sum_low, expand_bias_gradient = expand_back(upstream_last, reduce_all, slope)
    expand_bias_gradient = expand_bias_gradient.reshape(2, inner)
    far, near = contract(sum_low, expand_all, 0, 1), contract(sum_low, expand_all, 0, 0)
    expand_terms = outer(both, [(second, after(sum_low, *far, *near))], depth)
    second_back, _ = collect(far, near, expand_terms)
    expand_part = scatter(expand_terms, ("z", "c"))
    second_back = lax.optimization_barrier((*second_back, expand_terms))[:6]
    middle_back, sums_second, *middle_own = over_rows(
        middle_back_kernel,
        second_back,
        (middle, cotangent, live_wide),
        (row(gamma_second),),
        (F32,),
        pieces=2,
        sums=True,
    )
    active_last = after(activated, *middle_own)
    far, near = contract(active_last, reduce_all, 0, 1), contract(active_last, reduce_all, 0, 0)
    middle_low = spread_on(spread_out(*middle_own))
    terms = lax.optimization_barrier((*far, *near, middle_low))
    branch, moved = collect(terms[:2], terms[2:4])

    mixed_back = project(after(middle_low, reduce_part, *far, *near), heads_all, part, 3)
    projected_back = attend_back(info_two, projected, mixed_back, log_sums, block)
    heads_terms = outer(both, [(first, after(projected_back, *moved)), (middle_low, mixed)], depth)
    heads_part = scatter(heads_terms, ("z", "c"))
    far = contract(after(projected_back, heads_terms), heads_all, 0, 1)
    near = contract(after(projected_back, *far), heads_all, 0, 0)
    first_back, _ = collect(far, near)
    (outputs,) = over_rows(output_kernel, branch, (middle, live_wide), (row(reduce_bias),), (BF,))
    outputs = from_owner(outputs)
    input_gradient, sums_first = over_rows(
        input_back_kernel, first_back, (inputs, middle_back), (row(gamma_first),), (BF,), sums=True
    )
    input_gradient = from_owner(input_gradient)

    feed_got = shuffle(part_rows(plane_flag, reduce_part, expand_part), *first_back)
    reduce_gradient, expand_gradient = place(plane_flag, feed_got, 1, F32, (1, 1))
    gamma_first_gradient, beta_first_gradient = sums_first[0], sums_first[1]
    gamma_second_gradient, beta_second_gradient = sums_second[0], sums_second[1]
    output_bias_gradient, reduce_bias_gradient = sums_second[2], sums_second[3]

    vectors = jnp.stack(
        [
            gamma_first_gradient,
            beta_first_gradient,
            output_bias_gradient,
            gamma_second_gradient,
            beta_second_gradient,
            reduce_bias_gradient,
        ]
    )
    vectors = jnp.where(own, vectors, 0.0)
    placed = lax.dynamic_update_slice(jnp.zeros((2, 4 * inner), F32), expand_bias_gradient, (0, plane * inner))
    sums = jnp.concatenate([vectors.reshape(-1), placed.reshape(-1)]).reshape(-1, 128)
    for route in (
        lambda y, x, c: (y, x, 1 - c),
        lambda y, x, c: (y, 1 - x, c),
        lambda y, x, c: (1 - y, x, c),
    ):
        sums = sums + send(sums, route)
    step = 1
    while step < depth:
        sums = sums + lax.ppermute(sums, "z", [(i, i ^ step) for i in range(depth)])
        step *= 2
    flat = sums.reshape(-1)
    index = zi * 4 + plane
    vectors = lax.dynamic_slice_in_dim(flat[: 6 * model].reshape(6, model), index * shard, shard, axis=1)
    placed = flat[6 * model :].reshape(2, 4 * inner)
    count = 4 * inner // (4 * depth)
    expand_bias_gradient = lax.dynamic_slice(placed, (ci, index * count), (1, count))
    heads_part, reduce_gradient, expand_gradient, outputs, input_gradient, vectors, expand_bias_gradient = (
        lax.optimization_barrier(
            (heads_part, reduce_gradient, expand_gradient, outputs, input_gradient, vectors, expand_bias_gradient)
        )
    )
    heads_got = shuffle(part_rows(plane_flag, heads_part))
    heads_gradient, output_gradient = place(plane_flag, heads_got, 1, F32, (3, 1))
    heads_gradient = heads_gradient.transpose(1, 0, 2)
    return (
        outputs,
        input_gradient,
        vectors[0],
        vectors[1],
        heads_gradient,
        output_gradient,
        vectors[2],
        vectors[3],
        vectors[4],
        expand_gradient,
        expand_bias_gradient,
        reduce_gradient,
        vectors[5],
    )


def solution(mesh):
    depth = mesh.shape["dp"] // 4
    fine = Mesh(mesh.devices.reshape(depth, 2, 2, 2), ALL)
    dp = ("z", "y", "x")
    placed = (
        P(dp, None),
        P(),
        P(),
        P(dp, None, "c"),
        P(dp, "c"),
        P(),
        P(),
        P(),
        P(dp, "c"),
        P("c"),
        P(dp, "c"),
        P(),
        P(dp),
        P(dp),
        P(dp, None),
        P(dp, None),
    )
    return jax.shard_map(
        functools.partial(body, depth),
        mesh=fine,
        in_specs=placed,
        out_specs=(
            P(dp, None),
            P(dp, None),
            P(dp),
            P(dp),
            P(dp, None, "c"),
            P(dp, "c"),
            P(dp),
            P(dp),
            P(dp),
            P(dp, "c"),
            P("c", dp),
            P(dp, "c"),
            P(dp),
        ),
        check_vma=False,
    )
```

```python
import functools

import jax
import jax.numpy as jnp
from jax import lax
from jax.experimental import pallas as pl
from jax.experimental.pallas import tpu as pltpu
from jax.sharding import Mesh
from jax.sharding import PartitionSpec as P

HEAD = 128
WINDOW = 256
CHUNK = 128
SCALE = HEAD**-0.5
ALL = ("z", "y", "x", "c")
BF = jnp.bfloat16
F32 = jnp.float32
ACROSS = (((1,), (1,)), ((), ()))
ROWS = (((0,), (0,)), ((), ()))
PLAIN = (((1,), (0,)), ((), ()))


def dot(a, b, dims=PLAIN):
    return lax.dot_general(a, b, dims, preferred_element_type=F32)


def pairs_of(depth, route):
    def flat(z, y, x, c):
        return ((z * 2 + y) * 2 + x) * 2 + c

    found = []
    for z in range(depth):
        for y in range(2):
            for x in range(2):
                for c in range(2):
                    goal = route(y, x, c)
                    if goal is not None:
                        found.append((flat(z, y, x, c), flat(z, *goal)))
    return found


def bounds_of(group_sizes, prefix_lengths, solution_lengths, row_count):
    entries = solution_lengths.shape[1]
    position = jnp.arange(entries, dtype=jnp.int32)
    counted = jnp.where(position[None, :] < group_sizes[:, None], solution_lengths, 0)
    pieces = jnp.concatenate([prefix_lengths[:, None], counted], axis=1)
    flat = pieces.reshape(-1)
    count = flat.shape[0]
    index = jnp.arange(count, dtype=jnp.int32)
    ends = jnp.sum(jnp.where(index[None, :] <= index[:, None], flat[None, :], 0), axis=1)
    slot = jnp.arange(row_count, dtype=jnp.int32)
    passed = slot[:, None] >= ends[None, :]
    piece_start = jnp.max(jnp.where(passed, ends[None, :], 0), axis=1)
    group_end = ends.reshape(pieces.shape)[:, -1]
    over = slot[:, None] >= group_end[None, :]
    group_start = jnp.max(jnp.where(over, group_end[None, :], 0), axis=1)
    group_index = jnp.sum(over.astype(jnp.int32), axis=1)
    member = group_index[:, None] == jnp.arange(pieces.shape[0], dtype=jnp.int32)[None, :]
    prefix_end = group_start + jnp.sum(jnp.where(member, prefix_lengths[None, :], 0), axis=1)
    live = slot < ends[-1]
    piece_start = jnp.where(live, piece_start, slot)
    group_start = jnp.where(live, group_start, slot)
    prefix_end = jnp.where(live, prefix_end, slot)
    return jnp.stack([group_start, prefix_end, piece_start], axis=1), live


def key_range(i):
    return max(0, i * CHUNK - WINDOW), (i + 1) * CHUNK


def allowed_tile(info, i, lo, hi):
    rows = info[i * CHUNK : (i + 1) * CHUNK, :]
    start, stop, piece = rows[:, 0:1], rows[:, 1:2], rows[:, 2:3]
    s = lax.broadcasted_iota(jnp.int32, (CHUNK, hi - lo), 0) + i * CHUNK
    t = lax.broadcasted_iota(jnp.int32, (CHUNK, hi - lo), 1) + lo
    return (t <= s) & ((t >= piece) | ((t >= start) & (t < stop)))


def tiles_of(p_ref, width):
    found = []
    for i in range(p_ref.shape[0] // CHUNK):
        lo, hi = key_range(i)
        rows = slice(i * CHUNK, (i + 1) * CHUNK)
        for h in range(width // HEAD):
            qs, ks, vs = (slice(c * width + h * HEAD, c * width + (h + 1) * HEAD) for c in range(3))
            found.append((i, rows, slice(lo, hi), qs, ks, vs))
    return found


def masks_of(info_ref, block):
    info = info_ref[...]
    return [allowed_tile(info, i, *key_range(i)) for i in range(block // CHUNK)]


def attend_kernel(info_ref, p_ref, o_ref, l_ref):
    block, width = p_ref.shape
    width = width // 3
    masks = masks_of(info_ref, block)
    tiles = tiles_of(p_ref, width)
    raw = [dot(p_ref[rows, qs], p_ref[keys, ks], ACROSS) for _, rows, keys, qs, ks, _ in tiles]
    low = []
    for (i, rows, _, qs, _, _), score in zip(tiles, raw):
        scores = jnp.where(masks[i], score * SCALE, -1e30)
        peak = jnp.max(scores, axis=-1, keepdims=True)
        e = jnp.exp(scores - peak)
        total = jnp.sum(e, axis=-1, keepdims=True)
        low.append((e * (1.0 / total)).astype(BF))
        l_ref[rows, qs] = jnp.broadcast_to(peak + jnp.log(total), (CHUNK, HEAD))
    for (_, rows, keys, qs, _, vs), soft in zip(tiles, low):
        o_ref[rows, qs] = dot(soft, p_ref[keys, vs]).astype(BF)


def attend_back_kernel(info_ref, p_ref, g_ref, l_ref, d_ref, dk_ref, dv_ref):
    block, width = p_ref.shape
    width = width // 3
    masks = masks_of(info_ref, block)
    tiles = tiles_of(p_ref, width)
    dk_ref[...] = jnp.zeros_like(dk_ref)
    dv_ref[...] = jnp.zeros_like(dv_ref)
    raw = [dot(p_ref[rows, qs], p_ref[keys, ks], ACROSS) for _, rows, keys, qs, ks, _ in tiles]
    tangents = [dot(g_ref[rows, qs], p_ref[keys, vs], ACROSS) for _, rows, keys, qs, _, vs in tiles]
    kept = []
    for (i, rows, _, qs, _, _), score, tangent in zip(tiles, raw, tangents):
        scores = jnp.where(masks[i], score * SCALE, -1e30)
        soft = jnp.exp(scores - l_ref[rows, qs.start : qs.start + 1])
        back = soft * tangent
        low = (back - soft * jnp.sum(back, axis=-1, keepdims=True)).astype(BF)
        kept.append((soft.astype(BF), low))
    for (_, rows, keys, qs, ks, _), (soft, low) in zip(tiles, kept):
        d_ref[rows, qs] = (dot(low, p_ref[keys, ks]) * SCALE).astype(BF)
        dk_ref[keys, qs] += dot(low, p_ref[rows, qs], ROWS)
        dv_ref[keys, qs] += dot(soft, g_ref[rows, qs], ROWS)
    d_ref[:, width : 2 * width] = (dk_ref[...] * SCALE).astype(BF)
    d_ref[:, 2 * width :] = dv_ref[...].astype(BF)


def params(mib=48):
    return pltpu.CompilerParams(vmem_limit_bytes=mib << 20)


def cost(flops, moved, exps=0):
    return pl.CostEstimate(flops=flops * 4, bytes_accessed=moved * 4, transcendentals=exps)


def attend(info, projected, block):
    sides, rows, width = projected.shape
    spec = lambda n: pl.BlockSpec((None, block, n), lambda b, c: (c, b, 0))
    return pl.pallas_call(
        attend_kernel,
        grid=(rows // block, sides),
        in_specs=[pl.BlockSpec((block, info.shape[1]), lambda b, c: (b, 0)), spec(width)],
        out_specs=[spec(width // 3)] * 2,
        out_shape=[jax.ShapeDtypeStruct((sides, rows, width // 3), t) for t in (BF, F32)],
        compiler_params=params(16),
        cost_estimate=cost(16 * rows * block * width, 8 * rows * width * 2, rows * block * 4),
        name="attend",
    )(info, projected)


def attend_back(info, projected, mixed_back, log_sums, block):
    sides, rows, width = projected.shape
    spec = lambda n: pl.BlockSpec((None, block, n), lambda b, c: (c, b, 0))
    return pl.pallas_call(
        attend_back_kernel,
        grid=(rows // block, sides),
        in_specs=[pl.BlockSpec((block, info.shape[1]), lambda b, c: (b, 0)), spec(width), spec(width // 3), spec(width // 3)],
        out_specs=spec(width),
        out_shape=jax.ShapeDtypeStruct((sides, rows, width), BF),
        scratch_shapes=[pltpu.VMEM((block, width // 3), F32)] * 2,
        compiler_params=params(20),
        cost_estimate=cost(40 * rows * block * width, 16 * rows * width * 2, rows * block * 4),
        name="attend_back",
    )(info, projected, mixed_back, log_sums)


def steps(width, step=256):
    return [slice(j, min(j + step, width)) for j in range(0, width, step)]


def far_away(v):
    return pltpu.with_memory_space_constraint(v, pltpu.HBM)


def project_kernel(a_ref, w_ref, o_ref):
    for s in steps(w_ref.shape[1]):
        o_ref[:, s] = dot(a_ref[...], w_ref[:, s]).astype(BF)


def project(rows, weights, width, column):
    m, k = rows.shape
    sides = weights.shape[0]
    return pl.pallas_call(
        project_kernel,
        grid=(sides,),
        in_specs=[pl.BlockSpec((m, k), lambda c: (0, 0)), pl.BlockSpec((None, k, width), lambda c: (c, 0, column))],
        out_specs=pl.BlockSpec((None, m, width), lambda c: (c, 0, 0)),
        out_shape=jax.ShapeDtypeStruct((sides, m, width), BF),
        compiler_params=params(24),
        cost_estimate=cost(2 * sides * m * k * width, 2 * (m * k + sides * k * width + sides * m * width)),
        name="project",
    )(far_away(rows), far_away(weights))


def expand_kernel(a_ref, w_ref, b_ref, o_ref, d_ref):
    root, cubic = 0.7978845608028654, 0.044715
    for s in steps(w_ref.shape[1]):
        v = dot(a_ref[...], w_ref[:, s]) + b_ref[:, s]
        square = v * v
        t = jnp.tanh(v * (root + root * cubic * square))
        half = 0.5 + 0.5 * t
        o_ref[:, s] = (v * half).astype(BF)
        d_ref[:, s] = half + v * (half * (1.0 - t)) * (root + 3.0 * root * cubic * square)


def expand(rows, weights, bias):
    m, k = rows.shape
    sides, _, n = weights.shape
    tile = min(n, 256)
    out = pl.BlockSpec((None, m, tile), lambda c, j: (c, 0, j))
    return pl.pallas_call(
        expand_kernel,
        grid=(sides, n // tile),
        in_specs=[
            pl.BlockSpec((m, k), lambda c, j: (0, 0)),
            pl.BlockSpec((None, k, tile), lambda c, j: (c, 0, j)),
            pl.BlockSpec((None, 1, tile), lambda c, j: (c, 0, j)),
        ],
        out_specs=[out, out],
        out_shape=[jax.ShapeDtypeStruct((sides, m, n), BF), jax.ShapeDtypeStruct((sides, m, n), F32)],
        compiler_params=params(24),
        cost_estimate=cost(2 * sides * m * k * n, 2 * (m * k + sides * k * n) + 6 * sides * m * n, sides * m * n),
        name="expand",
    )(far_away(rows), far_away(weights), bias)


def expand_back_kernel(a_ref, w_ref, d_ref, o_ref, s_ref):
    for s in steps(w_ref.shape[1]):
        back = dot(a_ref[...], w_ref[:, s]) * d_ref[:, s]
        o_ref[:, s] = back.astype(BF)
        s_ref[:, s] = jnp.sum(back, axis=0, keepdims=True)


def expand_back(rows, weights, slope):
    m, k = rows.shape
    sides, _, n = weights.shape
    tile = min(n, 512)
    out = pl.BlockSpec((None, m, tile), lambda c, j: (c, 0, j))
    return pl.pallas_call(
        expand_back_kernel,
        grid=(sides, n // tile),
        in_specs=[
            pl.BlockSpec((m, k), lambda c, j: (0, 0)),
            pl.BlockSpec((None, k, tile), lambda c, j: (c, 0, j)),
            out,
        ],
        out_specs=[out, pl.BlockSpec((None, 1, tile), lambda c, j: (c, 0, j))],
        out_shape=[jax.ShapeDtypeStruct((sides, m, n), BF), jax.ShapeDtypeStruct((sides, 1, n), F32)],
        compiler_params=params(24),
        cost_estimate=cost(2 * sides * m * k * n, 2 * (m * k + sides * k * n) + 6 * sides * m * n),
        name="expand_back",
    )(far_away(rows), far_away(weights), far_away(slope))


def contract_kernel(a_ref, w_ref, top_ref, low_ref):
    half = top_ref.shape[0]
    for s in steps(w_ref.shape[1]):
        total = dot(a_ref[0], w_ref[0, s, :], ACROSS)
        for c in range(1, a_ref.shape[0]):
            total = total + dot(a_ref[c], w_ref[c, s, :], ACROSS)
        top_ref[:, s] = total[:half].astype(BF)
        low_ref[:, s] = total[half:].astype(BF)


def contract(terms, weights, column, side):
    sides, m, n = terms.shape
    d = weights.shape[1]
    m = m // 2
    tile = min(d, 512)
    half = pl.BlockSpec((m // 2, tile), lambda j: (0, j))
    out = jax.ShapeDtypeStruct((m // 2, d), BF)
    return pl.pallas_call(
        contract_kernel,
        grid=(d // tile,),
        in_specs=[
            pl.BlockSpec((sides, m, n), lambda j: (0, side, 0)),
            pl.BlockSpec((sides, tile, n), lambda j: (0, j, column)),
        ],
        out_specs=[half, half],
        out_shape=[out, out],
        compiler_params=params(16),
        cost_estimate=cost(2 * sides * m * n * d, 2 * (sides * m * n + sides * n * d + m * d)),
        name="contract",
    )(terms, far_away(weights))


def outer_kernel(pairs, adds, pick_ref, *refs):
    o_ref = refs[-1]
    start = 0
    for i in range(pairs):
        a_ref, r_ref = refs[2 * i], refs[2 * i + 1]
        for s in steps(r_ref.shape[1]):
            place = slice(start + s.start, start + s.stop)
            total = dot(a_ref[...], r_ref[:, s], ROWS)
            if adds:
                total = total + refs[2 * pairs][:, place].astype(F32)
            o_ref[:, place] = total.astype(BF)
        start += r_ref.shape[1]


def outer(pick, pairs, depth, extra=None):
    m, d = pairs[0][0].shape
    sides = pick.shape[0]
    total = sum(r.shape[2] for _, r in pairs)
    tile = d // depth
    place = pl.BlockSpec((None, None, tile, total), lambda c, i, s: (i, c, 0, 0))
    specs, args = [], []
    for a, r in pairs:
        specs.append(pl.BlockSpec((m, tile), lambda c, i, s: (0, i)))
        specs.append(pl.BlockSpec((None, m, r.shape[2]), lambda c, i, s: (s[c], 0, 0)))
        args += [a, r]
    if extra is not None:
        specs.append(place)
        args.append(extra)
    return pl.pallas_call(
        functools.partial(outer_kernel, len(pairs), extra is not None),
        grid_spec=pltpu.PrefetchScalarGridSpec(
            num_scalar_prefetch=1, grid=(sides, depth), in_specs=specs, out_specs=place
        ),
        out_shape=pltpu.HBM((depth, sides, tile, total), BF),
        compiler_params=params(16),
        cost_estimate=cost(4 * sides * m * d * total, 4 * (m * d + sides * m * total + sides * d * total)),
        name="outer",
    )(pick, *args)


TILE = 128


def whole(v):
    return pl.BlockSpec((TILE, v.shape[1]), lambda i: (i, 0))


def vector(v):
    return pl.BlockSpec(v.shape, lambda i: (0, 0))


def halves(v):
    count = v.shape[0] // TILE
    return (
        pl.BlockSpec((TILE, v.shape[1]), lambda i: (jnp.minimum(i, count - 1), 0)),
        pl.BlockSpec((TILE, v.shape[1]), lambda i: (jnp.maximum(i - count, 0), 0)),
    )


def in_half(count, use):
    for side in range(2):
        pl.when(pl.program_id(0) // count == side)(functools.partial(use, side))


def total_of(terms, side):
    picked = [t[...].astype(F32) for t in terms[3 * side : 3 * side + 3]]
    return picked[0] + picked[1] + picked[2]


def unit(values):
    center = values - jnp.mean(values, axis=-1, keepdims=True)
    factor = lax.rsqrt(jnp.mean(center * center, axis=-1, keepdims=True) + 1e-05)
    return center * factor, factor


def unit_back(tangent, gain, xhat, factor):
    e = tangent * gain
    return factor * (
        e - jnp.mean(e, axis=-1, keepdims=True) - xhat * jnp.mean(e * xhat, axis=-1, keepdims=True)
    )


def add_sums(s_ref, rows):
    sums = jnp.concatenate([jnp.sum(r, axis=0, keepdims=True) for r in rows], axis=0)
    first = pl.program_id(0) == 0

    @pl.when(first)
    def _():
        s_ref[0 : len(rows), :] = sums

    @pl.when(jnp.logical_not(first))
    def _():
        s_ref[0 : len(rows), :] += sums


def first_kernel(count, x_ref, gain_ref, shift_ref, *outs):
    def use(side):
        xhat, _ = unit(x_ref[...].astype(F32))
        outs[side][...] = (xhat * gain_ref[...] + shift_ref[...]).astype(BF)

    in_half(count, use)


def middle_kernel(count, *refs):
    terms, (x_ref, bias_ref, gain_ref, shift_ref, m_ref), outs = refs[:6], refs[6:11], refs[11:]

    def use(side):
        middle = x_ref[...].astype(F32) + total_of(terms, side) + bias_ref[...]
        m_ref[...] = middle
        xhat, _ = unit(middle)
        outs[side][...] = (xhat * gain_ref[...] + shift_ref[...]).astype(BF)

    in_half(count, use)


def output_kernel(count, *refs):
    terms, (m_ref, live_ref, bias_ref, o_ref) = refs[:6], refs[6:]

    def use(side):
        o_ref[...] = (live_ref[:, 0:1] * (m_ref[...] + total_of(terms, side) + bias_ref[...])).astype(BF)

    in_half(count, use)


def middle_back_kernel(count, *refs):
    terms, (m_ref, g_ref, live_ref, gain_ref, b_ref, s_ref), outs = refs[:6], refs[6:12], refs[12:]

    def use(side):
        tangent = total_of(terms, side)
        xhat, factor = unit(m_ref[...])
        upstream = live_ref[:, 0:1] * g_ref[...].astype(F32)
        back = upstream + unit_back(tangent, gain_ref[...], xhat, factor)
        b_ref[...] = back
        outs[side][...] = back.astype(BF)
        add_sums(s_ref, [tangent * xhat, tangent, back, upstream])

    in_half(count, use)


def input_back_kernel(count, *refs):
    terms, (x_ref, b_ref, gain_ref, o_ref, s_ref) = refs[:6], refs[6:]

    def use(side):
        tangent = total_of(terms, side)
        xhat, factor = unit(x_ref[...].astype(F32))
        o_ref[...] = (b_ref[...] + unit_back(tangent, gain_ref[...], xhat, factor)).astype(BF)
        add_sums(s_ref, [tangent * xhat, tangent])

    in_half(count, use)


def over_rows(kernel, terms, rows, vectors, wholes=(), pieces=0, sums=False):
    m = rows[0].shape[0]
    d = rows[0].shape[1]
    half = jax.ShapeDtypeStruct((m // 2, d), BF)
    upper, lower = halves(half)
    specs = [upper] * 3 + [lower] * 3 if terms else []
    specs += [whole(r) for r in rows] + [vector(v) for v in vectors]
    outs = [jax.ShapeDtypeStruct((m, d), t) for t in wholes]
    out_specs = [whole(o) for o in outs]
    if sums:
        outs.append(jax.ShapeDtypeStruct((8, d), F32))
        out_specs.append(vector(outs[-1]))
    outs += [half] * pieces
    out_specs += [upper, lower][:pieces]
    return pl.pallas_call(
        functools.partial(kernel, m // 2 // TILE),
        grid=(m // TILE,),
        in_specs=specs,
        out_specs=out_specs,
        out_shape=outs,
        compiler_params=params(24),
        cost_estimate=cost(20 * m * d, 16 * m * d),
        name=kernel.__name__.replace("_kernel", ""),
    )(*terms, *rows, *vectors)


def assemble_kernel(own_ref, *refs):
    pieces, o_ref, sems = refs[:8], refs[8], refs[9]
    rows = pieces[0].shape[0]
    for side in range(2):

        @pl.when(own_ref[0] == 1 - side)
        def _():
            copies = [
                pltpu.make_async_copy(pieces[4 * side + k], o_ref.at[pl.ds(k * rows, rows), :], sems.at[k])
                for k in range(4)
            ]
            for c in copies:
                c.start()
            for c in copies:
                c.wait()


def assemble(own, mine, theirs):
    rows, d = mine[0].shape
    anywhere = pl.BlockSpec(memory_space=pl.ANY)
    return pl.pallas_call(
        assemble_kernel,
        in_specs=[pl.BlockSpec(memory_space=pltpu.SMEM)] + [anywhere] * 8,
        out_specs=pl.BlockSpec(memory_space=pltpu.VMEM),
        out_shape=jax.ShapeDtypeStruct((4 * rows, d), BF),
        scratch_shapes=[pltpu.SemaphoreType.DMA((4,))],
        compiler_params=params(10),
        cost_estimate=cost(0, 16 * rows * d),
        name="assemble",
    )(own, *mine, *theirs)


def place_kernel(plane_ref, *refs):
    for k in range(4):

        @pl.when(pl.program_id(0) == k)
        def _():
            start = 0
            for o_ref in refs[4:]:
                if len(o_ref.shape) == 3:
                    width = o_ref.shape[2]
                    for j in range(o_ref.shape[0]):
                        o_ref[j] = refs[k][:, start : start + width].astype(o_ref.dtype)
                        start += width
                else:
                    width = o_ref.shape[1]
                    o_ref[...] = refs[k][:, start : start + width].astype(o_ref.dtype)
                    start += width


def place(plane, pieces, axis, dtype, split=(1,)):
    m, n = pieces[0].shape
    unit_width = n // sum(split)
    outs, specs = [], []
    for count in split:
        if axis == 0:
            outs.append(jax.ShapeDtypeStruct((4 * m, n), dtype))
            specs.append(pl.BlockSpec((m, n), lambda k, p: (p[0] ^ k, 0)))
        elif count == 1:
            outs.append(jax.ShapeDtypeStruct((m, 4 * unit_width), dtype))
            specs.append(pl.BlockSpec((m, unit_width), lambda k, p: (0, p[0] ^ k)))
        else:
            outs.append(jax.ShapeDtypeStruct((count, m, 4 * unit_width), dtype))
            specs.append(pl.BlockSpec((count, m, unit_width), lambda k, p: (0, 0, p[0] ^ k)))
    return pl.pallas_call(
        place_kernel,
        grid_spec=pltpu.PrefetchScalarGridSpec(
            num_scalar_prefetch=1,
            grid=(4,),
            in_specs=[pl.BlockSpec((m, n), lambda k, p: (0, 0))] * 4,
            out_specs=specs,
        ),
        out_shape=outs,
        compiler_params=params(12),
        cost_estimate=cost(0, 16 * m * n),
        name="place",
    )(plane, *pieces)


def part_kernel(plane_ref, *refs):
    inputs, outs = refs[:-4], refs[-4:]
    for k in range(4):

        @pl.when(pl.program_id(0) == k)
        def _():
            start = 0
            for v_ref in inputs:
                outs[k][:, start : start + v_ref.shape[1]] = v_ref[...]
                start += v_ref.shape[1]


def part_rows(plane, *arrays):
    m, n = arrays[0].shape[0] // 4, sum(v.shape[1] for v in arrays)
    return pl.pallas_call(
        part_kernel,
        grid_spec=pltpu.PrefetchScalarGridSpec(
            num_scalar_prefetch=1,
            grid=(4,),
            in_specs=[pl.BlockSpec((m, v.shape[1]), lambda k, p: (p[0] ^ k, 0)) for v in arrays],
            out_specs=[pl.BlockSpec((m, n), lambda k, p: (0, 0))] * 4,
        ),
        out_shape=[jax.ShapeDtypeStruct((m, n), BF)] * 4,
        compiler_params=params(12),
        cost_estimate=cost(0, 16 * m * n),
        name="part_rows",
    )(plane, *arrays)


def after(value, *others):
    return lax.optimization_barrier((value, *others))[0]


def body(
    depth,
    inputs,
    gamma_first,
    beta_first,
    heads_weight,
    output_weight,
    output_bias,
    gamma_second,
    beta_second,
    expand_weight,
    expand_bias,
    reduce_weight,
    reduce_bias,
    group_sizes,
    prefix_lengths,
    solution_lengths,
    cotangent,
):
    block, model = inputs.shape
    zi, yi, xi, ci = (lax.axis_index(a) for a in ALL)
    plane = yi * 2 + xi
    own = xi == ci
    send = lambda v, route: lax.ppermute(v, ALL, pairs_of(depth, route))
    wide = lambda v: v.astype(F32)

    def near_of(v):
        return send(v, lambda y, x, c: (y, x, c) if c == x else (y, 1 - x, 1 - c))

    def far_of(v):
        return send(v, lambda y, x, c: (1 - y, x, c) if c == x else (1 - y, 1 - x, 1 - c))

    flip_y = lambda y, x, c: (1 - y, x, c)
    owners_y = lambda y, x, c: (1 - y, x, c) if c == x else None
    others_y = lambda y, x, c: (1 - y, x, c) if c != x else None
    owners_x = lambda y, x, c: (y, 1 - x, c) if c == x else None
    others_x = lambda y, x, c: (y, 1 - x, c) if c != x else None

    def spread_out(top, low):
        y_low, x_top = send(low, owners_y), send(top, owners_x)
        return top, low, send(top, owners_y), y_low, x_top, send(low, owners_x)

    def spread_on(moved):
        top, low, y_top, y_low, x_top, x_low = moved
        far_low, far_top = send(y_low, owners_x), send(x_top, others_y)
        return assemble(own_flag, (top, low, y_top, y_low), (x_top, x_low, far_top, far_low))

    def collect(far, near, *work):
        far_top, far_low = far
        near_top, near_low = near
        by_y, to_far = send(far_top, flip_y), send(far_low, others_x)
        by_x = send(near_low, others_x)
        ahead_y, ahead_x, *_ = lax.optimization_barrier((to_far, by_y, *work))
        from_y = send((wide(far_low) + wide(ahead_y)).astype(BF), owners_y)
        from_x = send((wide(near_top) + wide(ahead_x)).astype(BF), others_x)
        return (near_top, from_x, by_y, near_low, by_x, from_y), (to_far, by_y)

    def from_owner(v):
        return jnp.where(own, v, send(v, lambda y, x, c: (y, x, 1 - c) if c == x else None))

    def shuffle(pieces, *first):
        routes = (
            lambda y, x, c: (y, 1 - x, c),
            lambda y, x, c: (1 - y, x, c),
            lambda y, x, c: (1 - y, 1 - x, c),
        )
        pieces = lax.optimization_barrier((*pieces, *first))[:4]
        return [pieces[0]] + [send(pieces[k], routes[k - 1]) for k in (1, 2, 3)]

    def columns(v, k):
        width = v.shape[-1] // 4
        return lax.dynamic_slice_in_dim(v, (plane ^ k) * width, width, axis=-1)

    def placed_rows(pieces):
        return place(plane_flag, pieces, 0, BF)[0]

    def gather(rows):
        full = lax.all_gather(rows, ("c", "z"), axis=0, tiled=True)
        return full.reshape(2, full.shape[0] // 2, full.shape[1])

    def scatter(terms, axes):
        return lax.psum_scatter(terms.reshape(-1, terms.shape[-1]), axes, scatter_dimension=0, tiled=True)

    pick = ci.astype(jnp.int32).reshape(1)
    plane_flag = plane.astype(jnp.int32).reshape(1)
    own_flag = own.astype(jnp.int32).reshape(1)
    row = lambda v: wide(v).reshape(1, -1)
    shard, _, local = heads_weight.shape
    part = local // 4
    inner = expand_weight.shape[1] // 4

    def attention_columns(k):
        heads = columns(heads_weight, k)
        return jnp.concatenate([heads[:, 0], heads[:, 1], heads[:, 2], columns(output_weight, k)], axis=1)

    heads_got = shuffle([attention_columns(k) for k in range(4)])
    heads_all = gather(placed_rows(heads_got))

    info, live = bounds_of(group_sizes, prefix_lengths, solution_lengths, block)
    info = jnp.pad(info, ((0, 0), (0, 5)))
    live_mask = wide(live)[:, None]
    live_wide = jnp.broadcast_to(live_mask, (block, 128))
    info_two = jnp.concatenate([near_of(info), far_of(info)], axis=0)
    first_own = over_rows(first_kernel, (), (inputs,), (row(gamma_first), row(beta_first)), pieces=2)
    first_own = lax.optimization_barrier((*first_own, *heads_got))[:2]
    first = spread_on(spread_out(*first_own))

    expand_got = shuffle([columns(expand_weight, k) for k in range(4)], first)
    expand_all = gather(placed_rows(expand_got))
    reduce_got = shuffle([columns(reduce_weight, k) for k in range(4)], *expand_got)
    reduce_rows = placed_rows(reduce_got)
    bias_mine = lax.dynamic_slice_in_dim(expand_bias, plane * inner, inner).reshape(1, 1, inner)
    bias_other = send(bias_mine, lambda y, x, c: (y, x, 1 - c))
    bias = wide(
        jnp.where(ci == 0, jnp.concatenate([bias_mine, bias_other]), jnp.concatenate([bias_other, bias_mine]))
    )
    upstream_own = (live_mask * wide(cotangent)).astype(BF)
    upstream_own = (upstream_own[: block // 2], upstream_own[block // 2 :])

    both = jnp.arange(2, dtype=jnp.int32)
    first, reduce_rows, bias = lax.optimization_barrier((first, reduce_rows, bias))
    reduce_all = gather(reduce_rows)
    projected = project(first, heads_all, 3 * part, 0)
    mixed, log_sums = attend(info_two, projected, block)
    far = contract(mixed, heads_all, 3, 1)
    attended, _ = collect(far, contract(after(mixed, *far), heads_all, 3, 0))
    middle, *second_own = over_rows(
        middle_kernel, attended, (inputs,), (row(output_bias), row(gamma_second), row(beta_second)), (F32,), pieces=2
    )
    second = spread_on(spread_out(*second_own))
    upstream_low = spread_on(spread_out(*lax.optimization_barrier((*upstream_own, second))[:2]))
    activated, slope = expand(second, expand_all, bias)
    reduce_terms = outer(both, [(upstream_low, activated)], depth)
    reduce_part = scatter(reduce_terms, ("z", "c"))

    slope, upstream_last, _ = lax.optimization_barrier((slope, upstream_low, reduce_terms))
    sum_low, expand_bias_gradient = expand_back(upstream_last, reduce_all, slope)
    expand_bias_gradient = expand_bias_gradient.reshape(2, inner)
    far, near = contract(sum_low, expand_all, 0, 1), contract(sum_low, expand_all, 0, 0)
    expand_terms = outer(both, [(second, after(sum_low, *far, *near))], depth)
    second_back, _ = collect(far, near, expand_terms)
    expand_part = scatter(expand_terms, ("z", "c"))
    second_back = lax.optimization_barrier((*second_back, expand_terms))[:6]
    middle_back, sums_second, *middle_own = over_rows(
        middle_back_kernel,
        second_back,
        (middle, cotangent, live_wide),
        (row(gamma_second),),
        (F32,),
        pieces=2,
        sums=True,
    )
    active_last = after(activated, *middle_own)
    far, near = contract(active_last, reduce_all, 0, 1), contract(active_last, reduce_all, 0, 0)
    middle_low = spread_on(spread_out(*middle_own))
    terms = lax.optimization_barrier((*far, *near, middle_low))
    branch, moved = collect(terms[:2], terms[2:4])

    mixed_back = project(after(middle_low, reduce_part, *far, *near), heads_all, part, 3)
    projected_back = attend_back(info_two, projected, mixed_back, log_sums, block)
    heads_terms = outer(both, [(first, after(projected_back, *moved)), (middle_low, mixed)], depth)
    heads_part = scatter(heads_terms, ("z", "c"))
    far = contract(after(projected_back, heads_terms), heads_all, 0, 1)
    near = contract(after(projected_back, *far), heads_all, 0, 0)
    first_back, _ = collect(far, near)
    (outputs,) = over_rows(output_kernel, branch, (middle, live_wide), (row(reduce_bias),), (BF,))
    outputs = from_owner(outputs)
    input_gradient, sums_first = over_rows(
        input_back_kernel, first_back, (inputs, middle_back), (row(gamma_first),), (BF,), sums=True
    )
    input_gradient = from_owner(input_gradient)

    feed_got = shuffle(part_rows(plane_flag, reduce_part, expand_part), *first_back)
    reduce_gradient, expand_gradient = place(plane_flag, feed_got, 1, F32, (1, 1))
    gamma_first_gradient, beta_first_gradient = sums_first[0], sums_first[1]
    gamma_second_gradient, beta_second_gradient = sums_second[0], sums_second[1]
    output_bias_gradient, reduce_bias_gradient = sums_second[2], sums_second[3]

    vectors = jnp.stack(
        [
            gamma_first_gradient,
            beta_first_gradient,
            output_bias_gradient,
            gamma_second_gradient,
            beta_second_gradient,
            reduce_bias_gradient,
        ]
    )
    vectors = jnp.where(own, vectors, 0.0)
    placed = lax.dynamic_update_slice(jnp.zeros((2, 4 * inner), F32), expand_bias_gradient, (0, plane * inner))
    sums = jnp.concatenate([vectors.reshape(-1), placed.reshape(-1)]).reshape(-1, 128)
    for route in (
        lambda y, x, c: (y, x, 1 - c),
        lambda y, x, c: (y, 1 - x, c),
        lambda y, x, c: (1 - y, x, c),
    ):
        sums = sums + send(sums, route)
    step = 1
    while step < depth:
        sums = sums + lax.ppermute(sums, "z", [(i, i ^ step) for i in range(depth)])
        step *= 2
    flat = sums.reshape(-1)
    index = zi * 4 + plane
    vectors = lax.dynamic_slice_in_dim(flat[: 6 * model].reshape(6, model), index * shard, shard, axis=1)
    placed = flat[6 * model :].reshape(2, 4 * inner)
    count = 4 * inner // (4 * depth)
    expand_bias_gradient = lax.dynamic_slice(placed, (ci, index * count), (1, count))
    heads_part, reduce_gradient, expand_gradient, outputs = lax.optimization_barrier(
        (heads_part, reduce_gradient, expand_gradient, outputs)
    )
    heads_got = shuffle(part_rows(plane_flag, heads_part))
    heads_gradient, output_gradient = place(plane_flag, heads_got, 1, F32, (3, 1))
    heads_gradient = heads_gradient.transpose(1, 0, 2)
    return (
        outputs,
        input_gradient,
        vectors[0],
        vectors[1],
        heads_gradient,
        output_gradient,
        vectors[2],
        vectors[3],
        vectors[4],
        expand_gradient,
        expand_bias_gradient,
        reduce_gradient,
        vectors[5],
    )


def solution(mesh):
    depth = mesh.shape["dp"] // 4
    fine = Mesh(mesh.devices.reshape(depth, 2, 2, 2), ALL)
    dp = ("z", "y", "x")
    placed = (
        P(dp, None),
        P(),
        P(),
        P(dp, None, "c"),
        P(dp, "c"),
        P(),
        P(),
        P(),
        P(dp, "c"),
        P("c"),
        P(dp, "c"),
        P(),
        P(dp),
        P(dp),
        P(dp, None),
        P(dp, None),
    )
    return jax.shard_map(
        functools.partial(body, depth),
        mesh=fine,
        in_specs=placed,
        out_specs=(
            P(dp, None),
            P(dp, None),
            P(dp),
            P(dp),
            P(dp, None, "c"),
            P(dp, "c"),
            P(dp),
            P(dp),
            P(dp),
            P(dp, "c"),
            P("c", dp),
            P(dp, "c"),
            P(dp),
        ),
        check_vma=False,
    )
```
